512 devices in a mesh: gx: 64 (over x, z), gy: 8 (over y, core).
Axes of the slice: x: 4, y: 4, z: 16, core: 2. Of those that a mesh axis runs over, the one named last changes fastest.
Arguments:
- u_old: bfloat16 [128, 16, 64, 128], P('gx', 'gy'), may hold values from -6 to 6
- rhs: bfloat16 [128, 16, 64, 128], P('gx', 'gy'), may hold values from -6 to 6
- classes: int32 [128, 16, 16], P('gx', 'gy'), may hold values from 0 to 7
- flags: int32 [2, 128, 16, 16], P(None, 'gx', 'gy'), may hold values from 0 to 1
- inverse: float32 [8, 64, 64], replicated, may hold values from -2 to 2
- x_face: float32 [8, 16, 16], replicated, may hold values from -2 to 2
- lateral_faces: float32 [4, 8, 16, 16], replicated, may hold values from -1.5 to 1.5
- inflow: float32 [16, 16, 128], P('gy'), may hold values from -6 to 6
Outputs:
- u_new: float32 [128, 16, 64, 128], P('gx', 'gy')
The draws below stay inside these ranges and needn't reach their ends.
All inputs are finite; a program needn't handle non-finite values.
Results may differ from the reference program's by a relative error of at most 0.0003.
Values may be sent and summed in bfloat16 or wider, within the bound.
A program may use at most 64 MiB of HBM per device.

```python
import math
import jax
import jax.numpy as jnp
from jax import lax

NODES = 64
FACE = 16
TRACERS = 8
NCLASS = 8
NZ = 16
NX = 128
NY = 16
COLS = 128


def basis_and_rates(key, slow_count):
    base = jax.random.fold_in(key, 9001)
    vector = jax.random.normal(jax.random.fold_in(base, 1), (FACE,), jnp.float32)
    basis = jnp.eye(FACE, dtype=jnp.float32) - 2.0 * jnp.outer(vector, vector) / jnp.sum(vector * vector)
    ranking = jax.random.permutation(jax.random.fold_in(base, 2), FACE)
    strength = jnp.exp(jax.random.uniform(jax.random.fold_in(base, 3), (FACE,), jnp.float32, math.log(0.8), math.log(2.2)))
    memory = jnp.exp(jax.random.uniform(jax.random.fold_in(base, 4), (FACE,), jnp.float32, math.log(30.0), math.log(50.0)))
    rates = jnp.where(ranking < slow_count, jnp.exp(-strength / NX), jnp.exp(-1.0 / memory))
    gains = jax.random.uniform(jax.random.fold_in(base, 5), (NCLASS, FACE), jnp.float32, 0.7, 1.3)
    losses = jnp.exp(-jax.random.uniform(jax.random.fold_in(base, 6), (NCLASS, 1), jnp.float32, 0.0, 0.5) / NX)
    return (basis, rates, gains, losses, ranking)


def group_masks(ranking):
    first = (ranking < FACE // 2).astype(jnp.float32)
    second = ((ranking >= FACE // 2) & (ranking < FACE - 2)).astype(jnp.float32)
    third = (ranking >= FACE - 2).astype(jnp.float32)
    return jnp.stack([first, second, third], axis=0)


def group_reflections(key, masks):
    vectors = jax.random.normal(key, (NCLASS, 3, FACE), jnp.float32) * masks[None]
    lengths = jnp.sum(vectors * vectors, axis=2, keepdims=True)
    outers = 2.0 * vectors[:, :, :, None] * vectors[:, :, None, :] / lengths[:, :, :, None]
    return jnp.eye(FACE, dtype=jnp.float32)[None] - jnp.sum(outers, axis=1)


def cross_rotations(key, masks):
    inside = jax.random.normal(jax.random.fold_in(key, 1), (NCLASS, FACE), jnp.float32) * masks[0][None]
    outside = jax.random.normal(jax.random.fold_in(key, 2), (NCLASS, FACE), jnp.float32) * (1.0 - masks[0])[None]
    inside = inside / jnp.sqrt(jnp.sum(inside * inside, axis=1, keepdims=True))
    outside = outside / jnp.sqrt(jnp.sum(outside * outside, axis=1, keepdims=True))
    angle = 0.07
    pair = inside[:, :, None] * inside[:, None, :] + outside[:, :, None] * outside[:, None, :]
    turn = outside[:, :, None] * inside[:, None, :] - inside[:, :, None] * outside[:, None, :]
    return jnp.eye(FACE, dtype=jnp.float32)[None] + (math.cos(angle) - 1.0) * pair + math.sin(angle) * turn


def class_bases(key):
    basis, rates, gains, losses, ranking = basis_and_rates(key, FACE // 2)
    base = jax.random.fold_in(key, 7777)
    masks = group_masks(ranking)
    right_factor = group_reflections(jax.random.fold_in(base, 1), masks)
    left_factor = jnp.einsum('kij,kjl->kil', group_reflections(jax.random.fold_in(base, 2), masks), cross_rotations(jax.random.fold_in(base, 3), masks), precision=lax.Precision.HIGHEST)
    right_basis = jnp.einsum('ij,kjm->kim', basis, right_factor, precision=lax.Precision.HIGHEST)
    left_basis = jnp.einsum('ij,kjm->kim', basis, left_factor, precision=lax.Precision.HIGHEST)
    return (left_basis, right_basis)


def draw_x_face(key, part):
    basis, rates, gains, losses, ranking = basis_and_rates(key, FACE // 2)
    left_basis, right_basis = class_bases(key)
    return -jnp.einsum('kim,km,klm->kil', right_basis, gains, right_basis, precision=lax.Precision.HIGHEST)


def draw_inverse(key, part):
    own = jax.random.fold_in(key, 4242)
    slow_count = FACE // 2
    spread = jnp.clip(0.0375 * jax.random.normal(jax.random.fold_in(own, 1), (NCLASS, NODES, NODES), jnp.float32), -0.15, 0.15)
    basis, rates, gains, losses, ranking = basis_and_rates(key, slow_count)
    left_basis, right_basis = class_bases(key)
    leading = jnp.exp(jax.random.uniform(jax.random.fold_in(own, 2), (NCLASS, NODES), jnp.float32, math.log(0.5), math.log(1.5)))
    identity = jnp.eye(NODES, dtype=jnp.float32)
    matrix = spread * (1.0 - identity) + leading[:, :, None] * identity
    row_scale = jnp.where(jnp.arange(NODES) >= NODES - FACE, 0.3, 1.0).astype(jnp.float32)
    matrix = matrix * row_scale[None, :, None]
    factors = rates[None, :] * losses / gains
    block = jnp.einsum('kim,km,klm->kil', left_basis, factors, right_basis, precision=lax.Precision.HIGHEST)
    return matrix.at[:, NODES - FACE:, :FACE].set(block)


def plant(array, rng, smallest, top_value):
    spot = [jax.random.randint(jax.random.fold_in(rng, axis), (), 0, length) for axis, length in enumerate(array.shape)]
    longest = array.shape.index(max(array.shape))
    next_to = spot[:longest] + [(spot[longest] + 1) % array.shape[longest]] + spot[longest + 1:]
    return array.at[tuple(spot)].set(smallest).at[tuple(next_to)].set(top_value)


def steps_of(key, shape, pieces, least, top_value):
    gain, own = 1.0, jax.random.fold_in(key, 6)
    for axis_at, parts in pieces:
        heights = jnp.exp(jax.random.uniform(jax.random.fold_in(own, axis_at), (parts,), jnp.float32, least / len(pieces), top_value / len(pieces)))
        gain = gain * jnp.repeat(heights, shape[axis_at] // parts).reshape([-1 if axis == axis_at else 1 for axis in range(len(shape))])
    return gain


def noise(key, shape, width, reach, shards=(), kind=jnp.bfloat16):
    values = jax.random.normal(key, shape, jnp.float32) * width
    if len(shards) > 0:
        values = steps_of(key, shape, shards, -0.22, 0.18) * values
    return jnp.clip(values, min=-reach, max=reach).astype(kind)


def setup_inputs(seed: int = 0) -> dict:
    splits = jax.random.split(jax.random.key(seed), 9)
    u_old = noise(splits[0], (NX, NY, NODES, COLS), 1.0, 6.0, ((0, 64), (1, 8)))
    rhs = noise(splits[1], (NX, NY, NODES, COLS), 1.0, 6.0, ((0, 64), (1, 8)))
    classes = plant(jax.random.randint(splits[2], (NX, NY, NZ), 0, NCLASS), jax.random.fold_in(splits[2], 1), 0, NCLASS - 1).astype(jnp.int32)
    flags = plant(jax.random.randint(splits[3], (2, NX, NY, NZ), 0, 2), jax.random.fold_in(splits[3], 1), 0, 1).astype(jnp.int32)
    inverse = draw_inverse(jax.random.fold_in(splits[8], 71), 0)
    x_face = draw_x_face(jax.random.fold_in(splits[8], 71), 0)
    lateral_faces = noise(splits[6], (4, NCLASS, FACE, FACE), FACE ** -0.5, 1.5, (), jnp.float32)
    inflow = noise(splits[7], (NY, FACE, COLS), 1.0, 6.0, ((0, 8),), jnp.float32)
    return {"u_old": u_old, "rhs": rhs, "classes": classes, "flags": flags, "inverse": inverse, "x_face": x_face, "lateral_faces": lateral_faces, "inflow": inflow}


HIGH = lax.Precision.HIGHEST


def face_traces(field):
    planes, rows_y, columns = field.shape[0], field.shape[1], field.shape[3]
    cube = field.reshape(planes, rows_y, 4, 4, 4, columns)
    y_low = cube[:, :, :, 0].reshape(planes, rows_y, 16, columns)
    y_high = cube[:, :, :, 3].reshape(planes, rows_y, 16, columns)
    z_low = cube[:, :, :, :, 0].reshape(planes, rows_y, 16, columns)
    z_high = cube[:, :, :, :, 3].reshape(planes, rows_y, 16, columns)
    return y_low, y_high, z_low, z_high


def along_z(trace, upward):
    planes, rows_y, columns = trace.shape[0], trace.shape[1], trace.shape[3]
    split = trace.reshape(planes, rows_y, 16, TRACERS, NZ)
    border = jnp.zeros((planes, rows_y, 16, TRACERS, 1), trace.dtype)
    if upward:
        moved = jnp.concatenate([border, split[..., :-1]], axis=4)
    else:
        moved = jnp.concatenate([split[..., 1:], border], axis=4)
    return moved.reshape(planes, rows_y, 16, columns)


def class_onehot(classes):
    labels = jnp.arange(NCLASS, dtype=jnp.int32)[:, None, None, None]
    return (classes[None] == labels).astype(jnp.float32)


def class_columns(onehot):
    count, planes, rows_y = onehot.shape[0], onehot.shape[1], onehot.shape[2]
    spread = jnp.broadcast_to(onehot[:, :, :, None, None, :], (count, planes, rows_y, 1, TRACERS, NZ))
    return spread.reshape(count, planes, rows_y, 1, TRACERS * NZ)


def flag_columns(flag):
    planes, rows_y = flag.shape[0], flag.shape[1]
    spread = jnp.broadcast_to(flag.astype(jnp.float32)[:, :, None, None, :], (planes, rows_y, 1, TRACERS, NZ))
    return spread.reshape(planes, rows_y, 1, TRACERS * NZ)


def lateral_rhs(rhs, u_old, below_row, above_row, class_cols, flags, lateral_faces):
    y_low, y_high, z_low, z_high = face_traces(u_old)
    from_below = jnp.concatenate([below_row, y_high[:, :-1]], axis=1).astype(jnp.float32)
    from_above = jnp.concatenate([y_low[:, 1:], above_row], axis=1).astype(jnp.float32)
    from_front = along_z(z_high, True).astype(jnp.float32)
    from_back = along_z(z_low, False).astype(jnp.float32)
    y_flag = flag_columns(flags[0])
    z_flag = flag_columns(flags[1])

    def couple(face_index, source, weight):
        every = jnp.einsum("kij,xyjc->kxyic", lateral_faces[face_index], source, precision=HIGH)
        return jnp.sum(every * class_cols, axis=0) * weight

    planes, rows_y, columns = rhs.shape[0], rhs.shape[1], rhs.shape[3]
    shape = (planes, rows_y, 4, 4, columns)
    cube = rhs.astype(jnp.float32).reshape(planes, rows_y, 4, 4, 4, columns)
    cube = cube.at[:, :, :, 0].add(-couple(0, from_below, 1.0 - y_flag).reshape(shape))
    cube = cube.at[:, :, :, 3].add(-couple(1, from_above, y_flag).reshape(shape))
    cube = cube.at[:, :, :, :, 0].add(-couple(2, from_front, 1.0 - z_flag).reshape(shape))
    cube = cube.at[:, :, :, :, 3].add(-couple(3, from_back, z_flag).reshape(shape))
    return cube.reshape(planes, rows_y, 64, columns)


def apply_inverse(matrices, source, class_cols):
    total = jnp.zeros(source.shape[:2] + (matrices.shape[1], source.shape[3]), jnp.float32)
    for class_id in range(NCLASS):
        total = total + class_cols[class_id] * jnp.einsum("ij,xyjc->xyic", matrices[class_id], source, precision=HIGH)
    return total


def pick(table, hot_plane):
    return jnp.einsum("kab,kyz->yzab", table, hot_plane, precision=HIGH)


def applied(selected, trace):
    return jnp.einsum("...yzab,...ybtz->...yatz", selected, trace, precision=HIGH)


def reference(u_old, rhs, classes, flags, inverse, x_face, lateral_faces, inflow):
    coupling = -jnp.einsum("kij,kjl->kil", inverse[:, :, :16], x_face, precision=HIGH)
    onehot = class_onehot(classes)
    cols_all = class_columns(onehot)
    edge_row = jnp.zeros((1, 1, 16, COLS), jnp.bfloat16)

    def plane(trace, items):
        u_plane, r_plane, hot_plane, cols_plane, flag_plane = items
        q_plane = lateral_rhs(r_plane[None], u_plane[None], edge_row, edge_row, cols_plane[:, None], flag_plane[:, None], lateral_faces)
        w_plane = apply_inverse(inverse, q_plane, cols_plane[:, None])[0]
        result = w_plane.reshape(NY, 64, TRACERS, NZ) + applied(pick(coupling, hot_plane), trace)
        return result[:, 48:], result.reshape(NY, 64, COLS)

    start = inflow.reshape(NY, 16, TRACERS, NZ)
    items = (u_old, rhs, jnp.moveaxis(onehot, 1, 0), jnp.moveaxis(cols_all, 1, 0), jnp.moveaxis(flags, 1, 0))
    _, solved = lax.scan(plane, start, items)
    return solved
```

```python
import functools

import jax
import jax.numpy as jnp
from jax import lax
from jax.experimental import pallas as pl
from jax.experimental.pallas import tpu as pltpu
from jax.sharding import PartitionSpec as P

MESH = pl.DeviceIdType.MESH
NCLASS = 8
NZ = 16
LANES = 128
F32 = jnp.float32
BF16 = jnp.bfloat16
HIGHEST = lax.Precision.HIGHEST


def gather_plan(ring):
    far = {16: (6, -6, 3, -3), 8: (3, -3)}.get(ring, ())
    steps = (1, -1) if ring > 2 else (1,)
    covered = {0} | {f % ring for f in far}
    relays = []
    for held in (0,) + tuple(f % ring for f in far[::-1]):
        for step in steps:
            target = (held + step) % ring
            if target not in covered:
                covered.add(target)
                relays.append((held, step))
    for held in (0,) + tuple(f % ring for f in far):
        for step in (2, -2):
            target = (held + step) % ring
            if target not in covered:
                covered.add(target)
                relays.append((held, step))
    assert covered == set(range(ring)), covered
    return far, relays


def iota(shape, axis):
    return lax.broadcasted_iota(jnp.int32, shape, axis)


def lanes_of(value, index):
    return jnp.take_along_axis(value, index, axis=1, mode="promise_in_bounds")


def spread(ref, row):
    return jnp.broadcast_to(ref[pl.ds(row, 1), :], (8, LANES))


def total_of(terms):
    while len(terms) > 1:
        terms = [sum(terms[i : i + 2]) for i in range(0, len(terms), 2)]
    return terms[0]


def high_low(value):
    high = value.astype(BF16)
    return high, (value - high.astype(F32)).astype(BF16)


def pick_class(stacked, rows, masks):
    result = stacked[0:rows]
    for k in range(1, NCLASS):
        result = jnp.where(masks[k], stacked[k * rows : (k + 1) * rows], result)
    return result


def kernel(
    xd, zd, yd,
    u_hbm, rhs_hbm, cls_hbm, flg_hbm, inv_hbm, xf_hbm, lat_hbm, inflow_hbm,
    out_ref,
    u_v, rhs_v, cls_v, flg_v, inv_v, xf_v, lat_v, inflow_v, halo,
    meta_in, meta, ih, il, mhl, tw, src, rh, wo,
    clsb, ob, tmp, ec, up, vp, px, xo, ex, xp, ent, tr1,
    local_sem, halo_ss, halo_rs, cls_ss, cls_rs, o_ss, o_rs, px_ss, px_rs, xo_ss, xo_rs,
):
    gx, gy = lax.axis_index("gx"), lax.axis_index("gy")
    x, z = gx // zd, lax.rem(gx, zd)

    def at(dx=0, dz=0, dy=0):
        gx_to = lax.rem(x + dx + xd, xd) * zd + lax.rem(z + dz + zd, zd)
        return (gx_to, lax.rem(gy + dy + yd, yd))

    far, relays = gather_plan(zd)
    barrier = pltpu.get_barrier_semaphore()
    peers = [at(dz=d) for d in range(1, zd)] + [at(dx=d) for d in range(1, xd)] + [at(dy=1), at(dy=-1)]
    for peer in peers:
        pl.semaphore_signal(barrier, inc=1, device_id=peer, device_id_type=MESH)

    loads = [
        pltpu.make_async_copy(a, b, local_sem.at[i])
        for i, (a, b) in enumerate(
            [(inv_hbm, inv_v), (lat_hbm, lat_v), (xf_hbm, xf_v), (cls_hbm, cls_v), (flg_hbm, flg_v), (u_hbm, u_v), (rhs_hbm, rhs_v), (inflow_hbm, inflow_v)]
        )
    ]
    for load in loads:
        load.start()

    meta_in[...] = jnp.zeros_like(meta_in)
    loads[3].wait()
    loads[4].wait()
    for p in range(2):
        for r in range(2):
            meta_in[pl.ds(p * 2 + r, 1), pl.ds(0, NZ)] = cls_v[p, pl.ds(r, 1), :].astype(F32)
            for f in range(2):
                meta_in[pl.ds(4 + f * 4 + p * 2 + r, 1), pl.ds(0, NZ)] = flg_v[f, p, pl.ds(r, 1), :].astype(F32)
    row, col = iota((LANES, LANES), 0), iota((LANES, LANES), 1)
    tile = ((row < NZ) & (row == (col & 15))).astype(BF16)
    meta[...] = jnp.dot(meta_in[...].astype(BF16), tile, preferred_element_type=F32)
    clsb[0] = jnp.concatenate([meta[pl.ds(0, 4), :] * 16.0, jnp.zeros((4, LANES), F32)], axis=0)

    loads[0].wait()
    loads[1].wait()
    loads[2].wait()
    inv_all = inv_v[...].reshape(NCLASS * 64, 64)
    ih_value, il_value = high_low(inv_all)
    ih[...] = ih_value.reshape(NCLASS, 64, 64)
    il[...] = il_value.reshape(NCLASS, 64, 64)
    node, slot = iota((64, LANES), 0), iota((64, LANES), 1)
    face, j = slot >> 4, slot & 15
    a, b = j >> 2, j & 3
    y_node = 16 * a + b
    wanted = jnp.where(face == 0, y_node, jnp.where(face == 1, y_node + 12, jnp.where(face == 2, 4 * j, jnp.where(face == 3, 4 * j + 3, jnp.where(face == 4, j, -1)))))
    faces_of = jnp.dot(inv_all, (node == wanted).astype(F32), precision=HIGHEST, preferred_element_type=F32)
    tables = jnp.concatenate([lat_v[...].reshape(4 * NCLASS * 16, 16), xf_v[...].reshape(NCLASS * 16, 16)], axis=0)
    source_slot, sj = iota((16, LANES), 1), iota((16, LANES), 0)

    def slot_face_and_j(s):
        y_face = jnp.where((s & 7) < 4, 1, 0)
        y_j = 4 * (s >> 3) + (s & 3)
        t = s - 32
        z_face = jnp.where((t & 3) == 3, 2, jnp.where((t & 3) == 0, 3, -1))
        z_j = t >> 2
        in_face = jnp.where(s < 32, y_face, jnp.where(s < 96, z_face, 4))
        in_j = jnp.where(s < 32, y_j, jnp.where(s < 96, z_j, s & 15))
        return in_face, in_j

    _, column_j = slot_face_and_j(source_slot)
    placed = jnp.dot(tables, (column_j == sj).astype(F32), precision=HIGHEST, preferred_element_type=F32)
    slot_face, _ = slot_face_and_j(iota((16, LANES), 1))
    lane16 = iota((16, LANES), 1)
    tw_value = jnp.zeros((16, LANES), F32)
    for k in range(NCLASS):
        blocks = []
        for f in range(5):
            start = (f * NCLASS + k) * 16
            blocks.append(jnp.where(slot_face == f, placed[start : start + 16], 0.0))
        blocks.append(jnp.zeros((48, LANES), F32))
        matrix = -jnp.dot(faces_of[k * 64 : (k + 1) * 64], jnp.concatenate(blocks, axis=0), precision=HIGHEST, preferred_element_type=F32)
        high, low = high_low(matrix)
        mhl[k, :, pl.ds(0, LANES)] = high
        mhl[k, :, pl.ds(LANES, LANES)] = low
        kept = jnp.where((lane16 >= 96) & (lane16 < 112), matrix[48:64], 0.0)
        tw_value = tw_value + pltpu.roll(kept, (16 * k - 96) % LANES, 1)
    tw[...] = tw_value

    loads[5].wait()
    loads[6].wait()
    loads[7].wait()
    pl.semaphore_wait(barrier, len(peers))

    cls_copies = [
        pltpu.make_async_remote_copy(clsb.at[0], clsb.at[d], cls_ss.at[d - 1], cls_rs.at[d - 1], device_id=at(dz=d), device_id_type=MESH)
        for d in range(1, zd)
    ]
    halo_copies = [
        pltpu.make_async_remote_copy(u_v.at[:, 1], halo.at[0], halo_ss.at[0], halo_rs.at[0], device_id=at(dy=1), device_id_type=MESH),
        pltpu.make_async_remote_copy(u_v.at[:, 0], halo.at[1], halo_ss.at[1], halo_rs.at[1], device_id=at(dy=-1), device_id_type=MESH),
    ]
    for copy in halo_copies + cls_copies:
        copy.start()

    lane64, node64 = iota((64, LANES), 1), iota((64, LANES), 0)
    lane_z = lane64 & 15
    node_c = node64 & 3
    for p in range(2):
        for r in range(2):
            columns = pl.ds(r * LANES, LANES)
            rh[p, :, columns] = rhs_v[p, r]
            own = u_v[p, r].astype(F32)
            z_flag = meta[pl.ds(8 + p * 2 + r, 1), :]
            front = jnp.where(lane_z > 0, pltpu.roll(own, 1, 1), 0.0) * (1.0 - z_flag)
            back = jnp.where(lane_z < 15, pltpu.roll(own, LANES - 1, 1), 0.0) * z_flag
            z_source = jnp.where(node_c == 3, front, jnp.where(node_c == 0, back, 0.0))
            src[p, pl.ds(32, 64), columns] = z_source.astype(BF16)
            src[p, pl.ds(96, 32), columns] = jnp.zeros((32, LANES), BF16)
    for copy in halo_copies:
        copy.wait()
    has_below = jnp.where(gy > 0, 1.0, 0.0)
    has_above = jnp.where(gy < yd - 1, 1.0, 0.0)
    sub8 = iota((8, LANES), 0)
    for p in range(2):
        for r in range(2):
            y_flag = meta[pl.ds(4 + p * 2 + r, 1), :]
            if r == 0:
                below, above = halo[0, p].astype(F32), u_v[p, 1].astype(F32)
                m_below, m_above = (1.0 - y_flag) * has_below, y_flag
            else:
                below, above = u_v[p, 0].astype(F32), halo[1, p].astype(F32)
                m_below, m_above = 1.0 - y_flag, y_flag * has_above
            pieces = []
            for a_ in range(4):
                pieces.append(jnp.where(sub8 < 4, above[16 * a_ : 16 * a_ + 8] * m_above, below[16 * a_ + 8 : 16 * a_ + 16] * m_below))
            src[p, pl.ds(0, 32), pl.ds(r * LANES, LANES)] = jnp.concatenate(pieces, axis=0).astype(BF16)

    inv_high_out = ih[:, 48:64, :].reshape(NCLASS * 16, 64)
    inv_low_out = il[:, 48:64, :].reshape(NCLASS * 16, 64)
    lat_out = mhl[:, 48:64, :].reshape(NCLASS * 16, 2 * LANES)

    def class_masks(p, r, rows):
        labels = jnp.broadcast_to(meta[pl.ds(p * 2 + r, 1), :], (rows, LANES))
        return [labels == float(k) for k in range(NCLASS)]

    for p in range(2):
        source = src[p]
        stacked = (
            jnp.dot(lat_out, jnp.concatenate([source, source], axis=0), preferred_element_type=F32)
            + jnp.dot(inv_high_out, rh[p], preferred_element_type=F32)
            + jnp.dot(inv_low_out, rh[p], preferred_element_type=F32)
        )
        for r in range(2):
            wo[p, r] = pick_class(stacked[:, r * LANES : (r + 1) * LANES], 16, class_masks(p, r, 16))

    def class_step(index_row, source_ref):
        base = jnp.broadcast_to(clsb[0, pl.ds(index_row, 1), :], (8, LANES)).astype(jnp.int32)
        low, high = [], []
        for m in range(16):
            value = spread(source_ref, m)
            low.append(lanes_of(tw[pl.ds(0, 8), :], base + m) * value)
            high.append(lanes_of(tw[pl.ds(8, 8), :], base + m) * value)
        return total_of(low), total_of(high)

    for r in range(2):
        low, high = class_step(2 + r, wo.at[0, r])
        ob[0, r, pl.ds(0, 8), :] = low + wo[1, r, pl.ds(0, 8), :]
        ob[0, r, pl.ds(8, 8), :] = high + wo[1, r, pl.ds(8, 8), :]

    def o_copy(held, step):
        to = (held + step) % zd
        return pltpu.make_async_remote_copy(ob.at[held], ob.at[to], o_ss.at[to - 1], o_rs.at[to - 1], device_id=at(dz=step), device_id_type=MESH)

    started = {}

    def send(held, step):
        copy = o_copy(held, step)
        copy.start()
        started[(held + step) % zd] = copy

    for f in far:
        send(0, f)
    for held, step in relays:
        if held == 0:
            send(0, step)

    def relay(offset):
        started[offset % zd].wait_recv()
        for held, step in relays:
            if held == offset % zd:
                send(held, step)

    for copy in cls_copies:
        copy.wait()
    lane8 = iota((8, LANES), 1)
    lane_unit, lane_low = lane8 >> 4, lane8 & 15

    def propagator(d, carry):
        for r in range(2):
            first = jnp.broadcast_to(clsb[d, pl.ds(r, 1), :], (8, LANES)).astype(jnp.int32) + lane_unit
            second = jnp.broadcast_to(clsb[d, pl.ds(2 + r, 1), :], (8, LANES)).astype(jnp.int32)
            for h in range(2):
                for half in range(2):
                    tmp[r, h, pl.ds(half * 8, 8), :] = lanes_of(tw[pl.ds(half * 8, 8), :], first + 8 * h)
            sums = [[[] for _ in range(2)] for _ in range(2)]
            for m in range(16):
                values = [spread(tmp.at[r, h], m) for h in range(2)]
                for half in range(2):
                    factor = lanes_of(tw[pl.ds(half * 8, 8), :], second + m)
                    for h in range(2):
                        sums[h][half].append(factor * values[h])
            for h in range(2):
                for half in range(2):
                    whole = total_of(sums[h][half])
                    for unit in range(8):
                        ec[d, r, 8 * h + unit, pl.ds(half * 8, 8), :] = lanes_of(whole, lane_low + 16 * unit)
        return carry

    def propagators(start, stop):
        lax.fori_loop(start, stop, propagator, 0)

    def unit_step(i, carry):
        d = lax.rem(z - i + zd, zd)
        for r in range(2):
            sums = [[[] for _ in range(2)] for _ in range(2)]
            for m in range(16):
                values = [spread(up.at[i, r, h], m) for h in range(2)]
                for half in range(2):
                    factor = ec[d, r, m, pl.ds(half * 8, 8), :]
                    for h in range(2):
                        sums[h][half].append(factor * values[h])
            for h in range(2):
                for half in range(2):
                    up[i + 1, r, h, pl.ds(half * 8, 8), :] = total_of(sums[h][half])
        return carry

    def full_planes(p, carry):
        source = src[p]
        both = jnp.concatenate([source, source], axis=0)
        stacked = (
            jnp.dot(mhl[...].reshape(NCLASS * 64, 2 * LANES), both, preferred_element_type=F32)
            + jnp.dot(ih[...].reshape(NCLASS * 64, 64), rh[p], preferred_element_type=F32)
            + jnp.dot(il[...].reshape(NCLASS * 64, 64), rh[p], preferred_element_type=F32)
        )
        for r in range(2):
            labels = jnp.broadcast_to(meta[pl.ds(p * 2 + r, 1), :], (64, LANES))
            out_ref[p, r] = pick_class(stacked[:, r * LANES : (r + 1) * LANES], 64, [labels == float(k) for k in range(NCLASS)])
        return carry

    propagators(0, zd)
    for f in far[::-1]:
        relay(f)
    for r in range(2):
        for h in range(2):
            units = iota((16, LANES), 1) >> 4
            up[0, r, h] = (iota((16, LANES), 0) == units + 8 * h).astype(F32)
    lax.fori_loop(0, zd, unit_step, 0)
    px_copies = [
        pltpu.make_async_remote_copy(up.at[zd], px.at[d - 1], px_ss.at[d - 1], px_rs.at[d - 1], device_id=at(dx=d), device_id_type=MESH)
        for d in range(1, xd)
    ]
    for copy in px_copies:
        copy.start()
    lax.fori_loop(0, 2, full_planes, 0)

    def expand(value_ref, slot):
        for r in range(2):
            for h in range(2):
                for half in range(2):
                    whole = value_ref[r, h, pl.ds(half * 8, 8), :]
                    for unit in range(8):
                        ex[slot, r, 8 * h + unit, pl.ds(half * 8, 8), :] = lanes_of(whole, lane_low + 16 * unit)

    expand(up.at[z], xd - 1)
    for copy in px_copies:
        copy.wait()

    def expand_slot(d, carry):
        expand(px.at[d], d)
        return carry

    lax.fori_loop(0, xd - 1, expand_slot, 0)

    def apply(factors, source, r):
        low, high = [], []
        for m in range(16):
            value = spread(source, m)
            low.append(factors[m, pl.ds(0, 8), :] * value)
            high.append(factors[m, pl.ds(8, 8), :] * value)
        return total_of(low), total_of(high)

    for d in range(1, zd):
        if d not in [f % zd for f in far]:
            started[d].wait_recv()
    vp[0] = jnp.zeros((2, 16, LANES), F32)

    def group_step(i, carry):
        d = lax.rem(z - i + zd, zd)
        for r in range(2):
            low, high = apply(ec.at[d, r], vp.at[i, r], r)
            vp[i + 1, r, pl.ds(0, 8), :] = low + ob[d, r, pl.ds(0, 8), :]
            vp[i + 1, r, pl.ds(8, 8), :] = high + ob[d, r, pl.ds(8, 8), :]
        return carry

    lax.fori_loop(0, zd, group_step, 0)
    xo_copies = [
        pltpu.make_async_remote_copy(vp.at[zd], xo.at[d - 1], xo_ss.at[d - 1], xo_rs.at[d - 1], device_id=at(dx=d), device_id_type=MESH)
        for d in range(1, xd)
    ]
    for copy in xo_copies:
        copy.start()
    xp[0] = inflow_v[...]
    for copy in xo_copies:
        copy.wait()

    def x_step(i, carry):
        d = x - i - 1
        for r in range(2):
            low, high = apply(ex.at[d, r], xp.at[i, r], r)
            xp[i + 1, r, pl.ds(0, 8), :] = low + xo[d, r, pl.ds(0, 8), :]
            xp[i + 1, r, pl.ds(8, 8), :] = high + xo[d, r, pl.ds(8, 8), :]
        return carry

    lax.fori_loop(0, x, x_step, 0)
    for r in range(2):
        low, high = apply(ex.at[xd - 1, r], xp.at[x, r], r)
        ent[r, pl.ds(0, 8), :] = low + vp[z, r, pl.ds(0, 8), :]
        ent[r, pl.ds(8, 8), :] = high + vp[z, r, pl.ds(8, 8), :]
    for r in range(2):
        low, high = class_step(r, ent.at[r])
        tr1[r, pl.ds(0, 8), :] = low + wo[0, r, pl.ds(0, 8), :]
        tr1[r, pl.ds(8, 8), :] = high + wo[0, r, pl.ds(8, 8), :]

    for p, trace in enumerate((ent, tr1)):
        high, low = high_low(jnp.concatenate([trace[0], trace[1]], axis=1))
        half = jnp.concatenate([jnp.zeros((96, 2 * LANES), BF16), high, low], axis=0)
        stacked = jnp.dot(mhl[...].reshape(NCLASS * 64, 2 * LANES), jnp.concatenate([half, half], axis=0), preferred_element_type=F32)
        for r in range(2):
            out_ref[p, r] = out_ref[p, r] + pick_class(stacked[:, r * LANES : (r + 1) * LANES], 64, class_masks(p, r, 64))

    for copy in started.values():
        copy.wait_send()


def solution(mesh):
    gxs, yd = mesh.shape["gx"], mesh.shape["gy"]
    zd = min(16, gxs // 2)
    xd = gxs // zd

    def on_device(u_old, rhs, classes, flags, inverse, x_face, lateral_faces, inflow):
        any_space = pl.BlockSpec(memory_space=pl.ANY)
        dma = pltpu.SemaphoreType.DMA
        return pl.pallas_call(
            functools.partial(kernel, xd, zd, yd),
            name="sweep",
            out_shape=jax.ShapeDtypeStruct((2, 2, 64, LANES), F32),
            in_specs=[any_space] * 8,
            out_specs=pl.BlockSpec(memory_space=pltpu.VMEM),
            scratch_shapes=[
                pltpu.VMEM((2, 2, 64, LANES), BF16),
                pltpu.VMEM((2, 2, 64, LANES), BF16),
                pltpu.VMEM((2, 2, NZ), jnp.int32),
                pltpu.VMEM((2, 2, 2, NZ), jnp.int32),
                pltpu.VMEM((NCLASS, 64, 64), F32),
                pltpu.VMEM((NCLASS, 16, 16), F32),
                pltpu.VMEM((4, NCLASS, 16, 16), F32),
                pltpu.VMEM((2, 16, LANES), F32),
                pltpu.VMEM((2, 2, 64, LANES), BF16),
                pltpu.VMEM((16, LANES), F32),
                pltpu.VMEM((16, LANES), F32),
                pltpu.VMEM((NCLASS, 64, 64), BF16),
                pltpu.VMEM((NCLASS, 64, 64), BF16),
                pltpu.VMEM((NCLASS, 64, 2 * LANES), BF16),
                pltpu.VMEM((16, LANES), F32),
                pltpu.VMEM((2, LANES, 2 * LANES), BF16),
                pltpu.VMEM((2, 64, 2 * LANES), BF16),
                pltpu.VMEM((2, 2, 16, LANES), F32),
                pltpu.VMEM((zd, 8, LANES), F32),
                pltpu.VMEM((zd, 2, 16, LANES), F32),
                pltpu.VMEM((2, 2, 16, LANES), F32),
                pltpu.VMEM((zd, 2, 16, 16, LANES), F32),
                pltpu.VMEM((zd + 1, 2, 2, 16, LANES), F32),
                pltpu.VMEM((zd + 1, 2, 16, LANES), F32),
                pltpu.VMEM((xd - 1, 2, 2, 16, LANES), F32),
                pltpu.VMEM((xd - 1, 2, 16, LANES), F32),
                pltpu.VMEM((xd, 2, 16, 16, LANES), F32),
                pltpu.VMEM((xd, 2, 16, LANES), F32),
                pltpu.VMEM((2, 16, LANES), F32),
                pltpu.VMEM((2, 16, LANES), F32),
                dma((8,)),
                dma((2,)),
                dma((2,)),
                dma((zd - 1,)),
                dma((zd - 1,)),
                dma((zd - 1,)),
                dma((zd - 1,)),
                dma((xd - 1,)),
                dma((xd - 1,)),
                dma((xd - 1,)),
                dma((xd - 1,)),
            ],
            compiler_params=pltpu.CompilerParams(collective_id=0, has_side_effects=True),
        )(u_old, rhs, classes, flags, inverse, x_face, lateral_faces, inflow)

    return jax.shard_map(
        on_device,
        mesh=mesh,
        in_specs=(
            P("gx", "gy", None, None),
            P("gx", "gy", None, None),
            P("gx", "gy", None),
            P(None, "gx", "gy", None),
            P(),
            P(),
            P(),
            P("gy", None, None),
        ),
        out_specs=P("gx", "gy", None, None),
        check_vma=False,
    )
```

```python
import functools

import jax
import jax.numpy as jnp
from jax import lax
from jax.experimental import pallas as pl
from jax.experimental.pallas import tpu as pltpu
from jax.sharding import PartitionSpec as P

MESH = pl.DeviceIdType.MESH
NCLASS = 8
NZ = 16
LANES = 128
F32 = jnp.float32
BF16 = jnp.bfloat16
HIGHEST = lax.Precision.HIGHEST


def gather_plan(ring):
    assert ring == 16
    far = (5, -5)
    near = (2, -2, 1, -1)
    own = [(0, step) for step in near]
    relays = {5: [(5, 3)] + [(5, step) for step in near], 11: [(11, step) for step in near]}
    covered = {0, 5, 11} | {(held + step) % ring for held, step in own + relays[5] + relays[11]}
    assert covered == set(range(ring)), covered
    return far, own, relays


def iota(shape, axis):
    return lax.broadcasted_iota(jnp.int32, shape, axis)


def lanes_of(value, index):
    return jnp.take_along_axis(value, index, axis=1, mode="promise_in_bounds")


def spread(ref, row):
    return jnp.broadcast_to(ref[pl.ds(row, 1), :], (8, LANES))


def total_of(terms):
    while len(terms) > 1:
        terms = [sum(terms[i : i + 2]) for i in range(0, len(terms), 2)]
    return terms[0]


def high_low(value):
    high = value.astype(BF16)
    return high, (value - high.astype(F32)).astype(BF16)


def pick_class(stacked, rows, masks):
    result = stacked[0:rows]
    for k in range(1, NCLASS):
        result = jnp.where(masks[k], stacked[k * rows : (k + 1) * rows], result)
    return result


def kernel(
    xd, zd, yd,
    u_hbm, rhs_hbm, cls_hbm, flg_hbm, inv_hbm, xf_hbm, lat_hbm, inflow_hbm,
    out_ref,
    u_v, rhs_v, cls_v, flg_v, inv_v, xf_v, lat_v, inflow_v, halo,
    meta_in, meta, ih, il, mhl, tw, c1s, t0s, pairs, src, rh, wo,
    clsb, ob, ec, up, vp, px, xo, ex, xp, ent, tr1,
    local_sem, halo_ss, halo_rs, cls_ss, cls_rs, o_ss, o_rs, px_ss, px_rs, xo_ss, xo_rs,
):
    gx, gy = lax.axis_index("gx"), lax.axis_index("gy")
    x, z = gx // zd, lax.rem(gx, zd)

    def at(dx=0, dz=0, dy=0):
        gx_to = lax.rem(x + dx + xd, xd) * zd + lax.rem(z + dz + zd, zd)
        return (gx_to, lax.rem(gy + dy + yd, yd))

    loads = [
        pltpu.make_async_copy(a, b, local_sem.at[i])
        for i, (a, b) in enumerate(
            [(cls_hbm, cls_v), (flg_hbm, flg_v), (u_hbm, u_v), (inv_hbm, inv_v), (lat_hbm, lat_v), (xf_hbm, xf_v), (rhs_hbm, rhs_v), (inflow_hbm, inflow_v)]
        )
    ]
    for load in loads:
        load.start()
    far, own_near, relays = gather_plan(zd)
    barrier = pltpu.get_barrier_semaphore()
    peers = [at(dy=1), at(dy=-1)] + [at(dz=d) for d in (1, -1, 2, -2, 3, -3, 5, -5)] + [at(dx=d) for d in range(1, xd)]
    for peer in peers:
        pl.semaphore_signal(barrier, inc=1, device_id=peer, device_id_type=MESH)

    meta_in[...] = jnp.zeros_like(meta_in)
    loads[0].wait()
    loads[1].wait()
    for p in range(2):
        for r in range(2):
            meta_in[pl.ds(p * 2 + r, 1), pl.ds(0, NZ)] = cls_v[p, pl.ds(r, 1), :].astype(F32)
            for f in range(2):
                meta_in[pl.ds(4 + f * 4 + p * 2 + r, 1), pl.ds(0, NZ)] = flg_v[f, p, pl.ds(r, 1), :].astype(F32)
    row, col = iota((LANES, LANES), 0), iota((LANES, LANES), 1)
    tile = ((row < NZ) & (row == (col & 15))).astype(BF16)
    meta_value = jnp.dot(meta_in[...].astype(BF16), tile, preferred_element_type=F32)
    meta[...] = meta_value
    pair = meta_value[0:2] * 8.0 + meta_value[2:4]
    clsb[0] = jnp.where(iota((1, LANES), 1) < NZ, pair[0:1], pair[1:2])

    loads[3].wait()
    loads[4].wait()
    loads[5].wait()
    inv_all = inv_v[...].reshape(NCLASS * 64, 64)
    ih_value, il_value = high_low(inv_all)
    ih[...] = ih_value.reshape(NCLASS, 64, 64)
    il[...] = il_value.reshape(NCLASS, 64, 64)
    node, slot = iota((64, LANES), 0), iota((64, LANES), 1)
    face, j = slot >> 4, slot & 15
    a, b = j >> 2, j & 3
    y_node = 16 * a + b
    wanted = jnp.where(face == 0, y_node, jnp.where(face == 1, y_node + 12, jnp.where(face == 2, 4 * j, jnp.where(face == 3, 4 * j + 3, jnp.where(face == 4, j, -1)))))
    faces_of = jnp.dot(inv_all, (node == wanted).astype(F32), precision=HIGHEST, preferred_element_type=F32)
    tables = jnp.concatenate([lat_v[...].reshape(4 * NCLASS * 16, 16), xf_v[...].reshape(NCLASS * 16, 16)], axis=0)
    source_slot, sj = iota((16, LANES), 1), iota((16, LANES), 0)

    def slot_face_and_j(s):
        y_face = jnp.where((s & 7) < 4, 1, 0)
        y_j = 4 * (s >> 3) + (s & 3)
        t = s - 32
        z_face = jnp.where((t & 3) == 3, 2, jnp.where((t & 3) == 0, 3, -1))
        z_j = t >> 2
        in_face = jnp.where(s < 32, y_face, jnp.where(s < 96, z_face, 4))
        in_j = jnp.where(s < 32, y_j, jnp.where(s < 96, z_j, s & 15))
        return in_face, in_j

    slot_face, column_j = slot_face_and_j(source_slot)
    placed = jnp.dot(tables, (column_j == sj).astype(F32), precision=HIGHEST, preferred_element_type=F32)
    tw_value = jnp.zeros((16, LANES), F32)
    for k in range(NCLASS):
        blocks = []
        for f in range(5):
            start = (f * NCLASS + k) * 16
            blocks.append(jnp.where(slot_face == f, placed[start : start + 16], 0.0))
        blocks.append(jnp.zeros((48, LANES), F32))
        matrix = -jnp.dot(faces_of[k * 64 : (k + 1) * 64], jnp.concatenate(blocks, axis=0), precision=HIGHEST, preferred_element_type=F32)
        high, low = high_low(matrix)
        mhl[k, :, pl.ds(0, LANES)] = high
        mhl[k, :, pl.ds(LANES, LANES)] = low
        kept = jnp.where((source_slot >= 96) & (source_slot < 112), matrix[48:64], 0.0)
        tw_value = tw_value + pltpu.roll(kept, (16 * k - 96) % LANES, 1)
    tw[...] = tw_value
    halves = [pl.ds(0, 8), pl.ds(8, 8)]

    loads[2].wait()
    loads[6].wait()
    loads[7].wait()
    lane64, node64 = iota((64, LANES), 1), iota((64, LANES), 0)
    lane_z = lane64 & 15
    node_c = node64 & 3
    for p in range(2):
        for r in range(2):
            columns = pl.ds(r * LANES, LANES)
            rh[p, :, columns] = rhs_v[p, r]
            own = u_v[p, r].astype(F32)
            z_flag = meta[pl.ds(8 + p * 2 + r, 1), :]
            front = jnp.where(lane_z > 0, pltpu.roll(own, 1, 1), 0.0) * (1.0 - z_flag)
            back = jnp.where(lane_z < 15, pltpu.roll(own, LANES - 1, 1), 0.0) * z_flag
            z_source = jnp.where(node_c == 3, front, jnp.where(node_c == 0, back, 0.0))
            src[p, pl.ds(32, 64), columns] = z_source.astype(BF16)
            src[p, pl.ds(96, 32), columns] = jnp.zeros((32, LANES), BF16)

    pl.semaphore_wait(barrier, len(peers))

    halo_copies = [
        pltpu.make_async_remote_copy(u_v.at[:, 1], halo.at[0], halo_ss.at[0], halo_rs.at[0], device_id=at(dy=1), device_id_type=MESH),
        pltpu.make_async_remote_copy(u_v.at[:, 0], halo.at[1], halo_ss.at[1], halo_rs.at[1], device_id=at(dy=-1), device_id_type=MESH),
    ]
    for copy in halo_copies:
        copy.start()

    def sender(buffer, send_sems, recv_sems):
        copies = {}

        def send(held, step):
            to = (held + step) % zd
            copies[to] = pltpu.make_async_remote_copy(buffer.at[held], buffer.at[to], send_sems.at[to - 1], recv_sems.at[to - 1], device_id=at(dz=step), device_id_type=MESH)
            copies[to].start()

        return copies, send

    cls_copies, send_cls = sender(clsb, cls_ss, cls_rs)
    o_copies, send_o = sender(ob, o_ss, o_rs)

    def send_own(send):
        for step in far:
            send(0, step)
        for held, step in own_near:
            send(held, step)

    def relay(copies, send, offset):
        copies[offset].wait_recv()
        for held, step in relays[offset]:
            send(held, step)

    send_own(send_cls)

    lane8 = iota((8, LANES), 1)
    pair_first, pair_second = ((lane8 >> 3) & 7) * 16, (lane8 & 7) * 16
    for m in range(16):
        for half in range(2):
            c1s[m, halves[half], :] = lanes_of(tw[halves[half], :], pair_second + m)
            t0s[m, halves[half], :] = lanes_of(tw[halves[half], :], pair_first + m)
    lane16 = iota((16, LANES), 1)

    def pair_product(jj, carry):
        sums = [[], []]
        for m in range(16):
            value = spread(t0s.at[jj], m)
            for half in range(2):
                sums[half].append(c1s[m, halves[half], :] * value)
        product = jnp.concatenate([total_of(sums[0]), total_of(sums[1])], axis=0)
        high = product.astype(BF16)
        rest = product - high.astype(F32)
        middle = rest.astype(BF16)
        low = (rest - middle.astype(F32)).astype(BF16)
        pairs[jj, :, pl.ds(0, LANES)] = jnp.where(lane16 < 64, high.astype(F32), middle.astype(F32)).astype(BF16)
        pairs[jj, :, pl.ds(LANES, LANES)] = jnp.where(lane16 < 64, low.astype(F32), 0.0).astype(BF16)
        return carry

    lax.fori_loop(0, 16, pair_product, 0)

    for copy in halo_copies:
        copy.wait()

    has_below = jnp.where(gy > 0, 1.0, 0.0)
    has_above = jnp.where(gy < yd - 1, 1.0, 0.0)
    sub8 = iota((8, LANES), 0)
    for p in range(2):
        for r in range(2):
            y_flag = meta[pl.ds(4 + p * 2 + r, 1), :]
            if r == 0:
                below, above = halo[0, p].astype(F32), u_v[p, 1].astype(F32)
                m_below, m_above = (1.0 - y_flag) * has_below, y_flag
            else:
                below, above = u_v[p, 0].astype(F32), halo[1, p].astype(F32)
                m_below, m_above = 1.0 - y_flag, y_flag * has_above
            pieces = []
            for a_ in range(4):
                pieces.append(jnp.where(sub8 < 4, above[16 * a_ : 16 * a_ + 8] * m_above, below[16 * a_ + 8 : 16 * a_ + 16] * m_below))
            src[p, pl.ds(0, 32), pl.ds(r * LANES, LANES)] = jnp.concatenate(pieces, axis=0).astype(BF16)

    inv_high_out = ih[:, 48:64, :].reshape(NCLASS * 16, 64)
    inv_low_out = il[:, 48:64, :].reshape(NCLASS * 16, 64)
    lat_out = mhl[:, 48:64, :].reshape(NCLASS * 16, 2 * LANES)

    def class_masks(p, r, rows):
        labels = jnp.broadcast_to(meta[pl.ds(p * 2 + r, 1), :], (rows, LANES))
        return [labels == float(k) for k in range(NCLASS)]

    for p in range(2):
        source = src[p]
        stacked = (
            jnp.dot(lat_out, jnp.concatenate([source, source], axis=0), preferred_element_type=F32)
            + jnp.dot(inv_high_out, rh[p], preferred_element_type=F32)
            + jnp.dot(inv_low_out, rh[p], preferred_element_type=F32)
        )
        for r in range(2):
            wo[p, r] = pick_class(stacked[:, r * LANES : (r + 1) * LANES], 16, class_masks(p, r, 16))

    def class_step(index_row, source_ref):
        base = (jnp.broadcast_to(meta[pl.ds(index_row, 1), :], (8, LANES)) * 16.0).astype(jnp.int32)
        sums = [[], []]
        for m in range(16):
            value = spread(source_ref, m)
            for half in range(2):
                sums[half].append(lanes_of(tw[halves[half], :], base + m) * value)
        return total_of(sums[0]), total_of(sums[1])

    for r in range(2):
        parts = class_step(2 + r, wo.at[0, r])
        for half in range(2):
            ob[0, r, halves[half], :] = parts[half] + wo[1, r, halves[half], :]

    send_own(send_o)
    for offset in relays:
        relay(cls_copies, send_cls, offset)

    def full_planes(p, carry):
        source = src[p]
        both = jnp.concatenate([source, source], axis=0)
        stacked = (
            jnp.dot(mhl[...].reshape(NCLASS * 64, 2 * LANES), both, preferred_element_type=F32)
            + jnp.dot(ih[...].reshape(NCLASS * 64, 64), rh[p], preferred_element_type=F32)
            + jnp.dot(il[...].reshape(NCLASS * 64, 64), rh[p], preferred_element_type=F32)
        )
        for r in range(2):
            labels = jnp.broadcast_to(meta[pl.ds(p * 2 + r, 1), :], (64, LANES))
            out_ref[p, r] = pick_class(stacked[:, r * LANES : (r + 1) * LANES], 64, [labels == float(k) for k in range(NCLASS)])
        return carry

    lax.fori_loop(0, 2, full_planes, 0)

    pair_rows = iota((64, LANES), 0)
    lane_low = lane8 & 15

    def propagators(slots):
        for d in slots:
            if d > 0 and d not in relays:
                cls_copies[d].wait_recv()
            hot = []
            for r in range(2):
                labels = lanes_of(jnp.broadcast_to(clsb[d], (8, LANES)), lane_low + 16 * r)
                hot.append((jnp.concatenate([labels] * 8, axis=0).astype(jnp.int32) == pair_rows).astype(F32).astype(BF16))
            one = jnp.concatenate(hot, axis=1)
            every = jnp.dot(pairs[...].reshape(256, 2 * LANES), jnp.concatenate([one, one, one, one], axis=0), preferred_element_type=F32)
            for r in range(2):
                ec[d, r] = every[:, r * LANES : (r + 1) * LANES].reshape(16, 16, LANES)

    propagators((0, 1, 15, 2, 14, 5, 11))
    for offset in relays:
        relay(o_copies, send_o, offset)
    propagators((4, 12, 6, 10, 3, 13, 7, 9, 8))

    def unit_step(i, carry):
        d = lax.rem(z - i + zd, zd)
        for r in range(2):
            sums = [[[] for _ in range(2)] for _ in range(2)]
            for m in range(16):
                values = [spread(up.at[i, r, h], m) for h in range(2)]
                for half in range(2):
                    factor = ec[d, r, m, halves[half], :]
                    for h in range(2):
                        sums[h][half].append(factor * values[h])
            for h in range(2):
                for half in range(2):
                    up[i + 1, r, h, halves[half], :] = total_of(sums[h][half])
        return carry

    for r in range(2):
        for h in range(2):
            up[0, r, h] = (iota((16, LANES), 0) == (lane16 >> 4) + 8 * h).astype(F32)
    lax.fori_loop(0, zd, unit_step, 0)

    px_copies = [
        pltpu.make_async_remote_copy(up.at[zd], px.at[d - 1], px_ss.at[d - 1], px_rs.at[d - 1], device_id=at(dx=d), device_id_type=MESH)
        for d in range(1, xd)
    ]
    for copy in px_copies:
        copy.start()

    def expand(value_ref, slot):
        for r in range(2):
            for h in range(2):
                for half in range(2):
                    whole = value_ref[r, h, halves[half], :]
                    for unit in range(8):
                        ex[slot, r, 8 * h + unit, halves[half], :] = lanes_of(whole, lane_low + 16 * unit)

    expand(up.at[z], xd - 1)

    def apply(factors, source):
        sums = [[], []]
        for m in range(16):
            value = spread(source, m)
            for half in range(2):
                sums[half].append(factors[m, halves[half], :] * value)
        return total_of(sums[0]), total_of(sums[1])

    for d in range(1, zd):
        if d not in relays:
            o_copies[d].wait_recv()
    vp[0] = jnp.zeros((2, 16, LANES), F32)

    def group_step(i, carry):
        d = lax.rem(z - i + zd, zd)
        for r in range(2):
            parts = apply(ec.at[d, r], vp.at[i, r])
            for half in range(2):
                vp[i + 1, r, halves[half], :] = parts[half] + ob[d, r, halves[half], :]
        return carry

    lax.fori_loop(0, zd, group_step, 0)
    xo_copies = [
        pltpu.make_async_remote_copy(vp.at[zd], xo.at[d - 1], xo_ss.at[d - 1], xo_rs.at[d - 1], device_id=at(dx=d), device_id_type=MESH)
        for d in range(1, xd)
    ]
    for copy in xo_copies:
        copy.start()
    for copy in px_copies:
        copy.wait()

    def expand_slot(d, carry):
        expand(px.at[d], d)
        return carry

    lax.fori_loop(0, xd - 1, expand_slot, 0)
    xp[0] = inflow_v[...]
    for copy in xo_copies:
        copy.wait()

    def x_step(i, carry):
        d = x - i - 1
        for r in range(2):
            parts = apply(ex.at[d, r], xp.at[i, r])
            for half in range(2):
                xp[i + 1, r, halves[half], :] = parts[half] + xo[d, r, halves[half], :]
        return carry

    lax.fori_loop(0, x, x_step, 0)
    for r in range(2):
        parts = apply(ex.at[xd - 1, r], xp.at[x, r])
        for half in range(2):
            ent[r, halves[half], :] = parts[half] + vp[z, r, halves[half], :]
    for r in range(2):
        parts = class_step(r, ent.at[r])
        for half in range(2):
            tr1[r, halves[half], :] = parts[half] + wo[0, r, halves[half], :]

    for p, trace in enumerate((ent, tr1)):
        high, low = high_low(jnp.concatenate([trace[0], trace[1]], axis=1))
        half_rows = jnp.concatenate([jnp.zeros((96, 2 * LANES), BF16), high, low], axis=0)
        stacked = jnp.dot(mhl[...].reshape(NCLASS * 64, 2 * LANES), jnp.concatenate([half_rows, half_rows], axis=0), preferred_element_type=F32)
        for r in range(2):
            out_ref[p, r] = out_ref[p, r] + pick_class(stacked[:, r * LANES : (r + 1) * LANES], 64, class_masks(p, r, 64))

    for copy in list(cls_copies.values()) + list(o_copies.values()):
        copy.wait_send()


def solution(mesh):
    gxs, yd = mesh.shape["gx"], mesh.shape["gy"]
    zd = min(16, gxs // 2)
    xd = gxs // zd

    def on_device(u_old, rhs, classes, flags, inverse, x_face, lateral_faces, inflow):
        any_space = pl.BlockSpec(memory_space=pl.ANY)
        dma = pltpu.SemaphoreType.DMA
        return pl.pallas_call(
            functools.partial(kernel, xd, zd, yd),
            name="sweep",
            out_shape=pltpu.VMEM((2, 2, 64, LANES), F32),
            in_specs=[any_space] * 8,
            out_specs=pl.BlockSpec(memory_space=pltpu.VMEM),
            scratch_shapes=[
                pltpu.VMEM((2, 2, 64, LANES), BF16),
                pltpu.VMEM((2, 2, 64, LANES), BF16),
                pltpu.VMEM((2, 2, NZ), jnp.int32),
                pltpu.VMEM((2, 2, 2, NZ), jnp.int32),
                pltpu.VMEM((NCLASS, 64, 64), F32),
                pltpu.VMEM((NCLASS, 16, 16), F32),
                pltpu.VMEM((4, NCLASS, 16, 16), F32),
                pltpu.VMEM((2, 16, LANES), F32),
                pltpu.VMEM((2, 2, 64, LANES), BF16),
                pltpu.VMEM((16, LANES), F32),
                pltpu.VMEM((16, LANES), F32),
                pltpu.VMEM((NCLASS, 64, 64), BF16),
                pltpu.VMEM((NCLASS, 64, 64), BF16),
                pltpu.VMEM((NCLASS, 64, 2 * LANES), BF16),
                pltpu.VMEM((16, LANES), F32),
                pltpu.VMEM((16, 16, LANES), F32),
                pltpu.VMEM((16, 16, LANES), F32),
                pltpu.VMEM((16, 16, 2 * LANES), BF16),
                pltpu.VMEM((2, LANES, 2 * LANES), BF16),
                pltpu.VMEM((2, 64, 2 * LANES), BF16),
                pltpu.VMEM((2, 2, 16, LANES), F32),
                pltpu.VMEM((zd, 1, LANES), F32),
                pltpu.VMEM((zd, 2, 16, LANES), F32),
                pltpu.VMEM((zd, 2, 16, 16, LANES), F32),
                pltpu.VMEM((zd + 1, 2, 2, 16, LANES), F32),
                pltpu.VMEM((zd + 1, 2, 16, LANES), F32),
                pltpu.VMEM((xd - 1, 2, 2, 16, LANES), F32),
                pltpu.VMEM((xd - 1, 2, 16, LANES), F32),
                pltpu.VMEM((xd, 2, 16, 16, LANES), F32),
                pltpu.VMEM((xd, 2, 16, LANES), F32),
                pltpu.VMEM((2, 16, LANES), F32),
                pltpu.VMEM((2, 16, LANES), F32),
                dma((8,)),
                dma((2,)),
                dma((2,)),
                dma((zd - 1,)),
                dma((zd - 1,)),
                dma((zd - 1,)),
                dma((zd - 1,)),
                dma((xd - 1,)),
                dma((xd - 1,)),
                dma((xd - 1,)),
                dma((xd - 1,)),
            ],
            compiler_params=pltpu.CompilerParams(collective_id=0, has_side_effects=True),
        )(u_old, rhs, classes, flags, inverse, x_face, lateral_faces, inflow)

    return jax.shard_map(
        on_device,
        mesh=mesh,
        in_specs=(
            P("gx", "gy", None, None),
            P("gx", "gy", None, None),
            P("gx", "gy", None),
            P(None, "gx", "gy", None),
            P(),
            P(),
            P(),
            P("gy", None, None),
        ),
        out_specs=P("gx", "gy", None, None),
        check_vma=False,
    )
```

```python
import functools

import jax
import jax.numpy as jnp
from jax import lax
from jax.experimental import pallas as pl
from jax.experimental.pallas import tpu as pltpu
from jax.sharding import PartitionSpec as P

MESH = pl.DeviceIdType.MESH
NCLASS = 8
NZ = 16
LANES = 128
F32 = jnp.float32
BF16 = jnp.bfloat16
HIGHEST = lax.Precision.HIGHEST


def gather_plan(ring):
    assert ring == 16
    far = (5, -5)
    near = (2, -2, 1, -1)
    own = [(0, step) for step in near]
    relays = {5: [(5, 3)] + [(5, step) for step in near], 11: [(11, step) for step in near]}
    covered = {0, 5, 11} | {(held + step) % ring for held, step in own + relays[5] + relays[11]}
    assert covered == set(range(ring)), covered
    return far, own, relays


def iota(shape, axis):
    return lax.broadcasted_iota(jnp.int32, shape, axis)


def lanes_of(value, index):
    return jnp.take_along_axis(value, index, axis=1, mode="promise_in_bounds")


def spread(ref, row):
    return jnp.broadcast_to(ref[pl.ds(row, 1), :], (8, LANES))


def total_of(terms):
    while len(terms) > 1:
        terms = [sum(terms[i : i + 2]) for i in range(0, len(terms), 2)]
    return terms[0]


def high_low(value):
    high = value.astype(BF16)
    return high, (value - high.astype(F32)).astype(BF16)


def pick_class(stacked, rows, masks):
    result = stacked[0:rows]
    for k in range(1, NCLASS):
        result = jnp.where(masks[k], stacked[k * rows : (k + 1) * rows], result)
    return result


def kernel(
    xd, zd, yd,
    u_hbm, rhs_hbm, cls_hbm, flg_hbm, inv_hbm, xf_hbm, lat_hbm, inflow_hbm,
    out_ref,
    u_v, rhs_v, cls_v, flg_v, inv_v, xf_v, lat_v, inflow_v, border, halo,
    meta_in, meta, ih, il, mhl, tw, c1s, t0s, pairs, src, rh, wo,
    clsb, ob, ec, up, vp, px, xo, ex, xp, ent, tr1,
    know, know_x, local_sem, halo_ss, halo_rs, cls_ss, cls_rs, o_ss, o_rs, px_ss, px_rs, xo_ss, xo_rs,
):
    gx, gy = lax.axis_index("gx"), lax.axis_index("gy")
    x, z = gx // zd, lax.rem(gx, zd)

    def at(dx=0, dz=0, dy=0):
        gx_to = lax.rem(x + dx + xd, xd) * zd + lax.rem(z + dz + zd, zd)
        return (gx_to, lax.rem(gy + dy + yd, yd))

    loads = [
        pltpu.make_async_copy(a, b, local_sem.at[i])
        for i, (a, b) in enumerate(
            [(cls_hbm, cls_v), (flg_hbm, flg_v), (u_hbm, u_v), (inv_hbm, inv_v), (lat_hbm, lat_v), (xf_hbm, xf_v), (rhs_hbm, rhs_v), (inflow_hbm, inflow_v)]
        )
    ]
    for load in loads:
        load.start()
    far, own_near, relays = gather_plan(zd)
    barrier = pltpu.get_barrier_semaphore()
    for peer in (at(dy=1), at(dy=-1)) + tuple(at(dz=d) for d in (1, -1, 2, -2, 3, -3)):
        pl.semaphore_signal(barrier, inc=1, device_id=peer, device_id_type=MESH)

    @pl.when(x > 0)
    def _():
        pl.semaphore_signal(barrier, inc=1, device_id=at(dx=-1), device_id_type=MESH)

    @pl.when(x < xd - 1)
    def _():
        pl.semaphore_signal(barrier, inc=1, device_id=at(dx=1), device_id_type=MESH)

    greeted = 8 + jnp.where(x > 0, 1, 0) + jnp.where(x < xd - 1, 1, 0)

    def tell(semaphore, step):
        for sign in (1, -1):
            pl.semaphore_signal(semaphore, inc=1, device_id=at(dz=sign * step), device_id_type=MESH)

    meta_in[...] = jnp.zeros_like(meta_in)
    loads[0].wait()
    loads[1].wait()
    for p in range(2):
        for r in range(2):
            meta_in[pl.ds(p * 2 + r, 1), pl.ds(0, NZ)] = cls_v[p, pl.ds(r, 1), :].astype(F32)
            for f in range(2):
                meta_in[pl.ds(4 + f * 4 + p * 2 + r, 1), pl.ds(0, NZ)] = flg_v[f, p, pl.ds(r, 1), :].astype(F32)
    row, col = iota((LANES, LANES), 0), iota((LANES, LANES), 1)
    tile = ((row < NZ) & (row == (col & 15))).astype(BF16)
    meta_value = jnp.dot(meta_in[...].astype(BF16), tile, preferred_element_type=F32)
    meta[...] = meta_value
    pair = meta_value[0:2] * 8.0 + meta_value[2:4]
    clsb[0] = jnp.where(iota((1, LANES), 1) < NZ, pair[0:1], pair[1:2])

    loads[2].wait()
    sub8 = iota((8, LANES), 0)
    top = [u_v[p, 1].astype(F32) for p in range(2)]
    bottom = [u_v[p, 0].astype(F32) for p in range(2)]
    packed_top, packed_bottom = [], []
    for a_ in range(4):
        low_rows, high_rows = slice(16 * a_, 16 * a_ + 8), slice(16 * a_ + 8, 16 * a_ + 16)
        packed_top.append(jnp.where(sub8 < 4, pltpu.roll(top[0][high_rows], 4, 0), top[1][high_rows]))
        packed_bottom.append(jnp.where(sub8 < 4, bottom[0][low_rows], pltpu.roll(bottom[1][low_rows], 4, 0)))
    border[0] = jnp.concatenate(packed_top, axis=0).astype(BF16)
    border[1] = jnp.concatenate(packed_bottom, axis=0).astype(BF16)
    pl.semaphore_wait(barrier, greeted)

    halo_copies = [
        pltpu.make_async_remote_copy(border.at[0], halo.at[0], halo_ss.at[0], halo_rs.at[0], device_id=at(dy=1), device_id_type=MESH),
        pltpu.make_async_remote_copy(border.at[1], halo.at[1], halo_ss.at[1], halo_rs.at[1], device_id=at(dy=-1), device_id_type=MESH),
    ]
    for copy in halo_copies:
        copy.start()
    tell(know.at[0], 2)

    @pl.when((x > 0) & (x < xd - 1))
    def _():
        pl.semaphore_signal(know_x.at[0], inc=1, device_id=at(dx=-1), device_id_type=MESH)

    def sender(buffer, send_sems, recv_sems):
        copies = {}

        def send(held, step):
            to = (held + step) % zd
            copies[to] = pltpu.make_async_remote_copy(buffer.at[held], buffer.at[to], send_sems.at[to - 1], recv_sems.at[to - 1], device_id=at(dz=step), device_id_type=MESH)
            copies[to].start()

        return copies, send

    cls_copies, send_cls = sender(clsb, cls_ss, cls_rs)
    o_copies, send_o = sender(ob, o_ss, o_rs)

    def send_own(send):
        for step in far:
            send(0, step)
        for held, step in own_near:
            send(held, step)

    for held, step in own_near:
        send_cls(held, step)

    def relay(copies, send, offset):
        copies[offset].wait_recv()
        for held, step in relays[offset]:
            send(held, step)

    loads[3].wait()
    loads[4].wait()
    loads[5].wait()
    inv_all = inv_v[...].reshape(NCLASS * 64, 64)
    ih_value, il_value = high_low(inv_all)
    ih[...] = ih_value.reshape(NCLASS, 64, 64)
    il[...] = il_value.reshape(NCLASS, 64, 64)
    node, slot = iota((64, LANES), 0), iota((64, LANES), 1)
    face, j = slot >> 4, slot & 15
    a, b = j >> 2, j & 3
    y_node = 16 * a + b
    wanted = jnp.where(face == 0, y_node, jnp.where(face == 1, y_node + 12, jnp.where(face == 2, 4 * j, jnp.where(face == 3, 4 * j + 3, jnp.where(face == 4, j, -1)))))
    faces_of = jnp.dot(inv_all, (node == wanted).astype(F32), precision=HIGHEST, preferred_element_type=F32)
    tables = jnp.concatenate([lat_v[...].reshape(4 * NCLASS * 16, 16), xf_v[...].reshape(NCLASS * 16, 16)], axis=0)
    source_slot, sj = iota((16, LANES), 1), iota((16, LANES), 0)

    def slot_face_and_j(s):
        y_face = jnp.where((s & 7) < 4, 1, 0)
        y_j = 4 * (s >> 3) + (s & 3)
        t = s - 32
        z_face = jnp.where((t & 3) == 3, 2, jnp.where((t & 3) == 0, 3, -1))
        z_j = t >> 2
        in_face = jnp.where(s < 32, y_face, jnp.where(s < 96, z_face, 4))
        in_j = jnp.where(s < 32, y_j, jnp.where(s < 96, z_j, s & 15))
        return in_face, in_j

    slot_face, column_j = slot_face_and_j(source_slot)
    placed = jnp.dot(tables, (column_j == sj).astype(F32), precision=HIGHEST, preferred_element_type=F32)
    tw_value = jnp.zeros((16, LANES), F32)
    for k in range(NCLASS):
        blocks = []
        for f in range(5):
            start = (f * NCLASS + k) * 16
            blocks.append(jnp.where(slot_face == f, placed[start : start + 16], 0.0))
        blocks.append(jnp.zeros((48, LANES), F32))
        matrix = -jnp.dot(faces_of[k * 64 : (k + 1) * 64], jnp.concatenate(blocks, axis=0), precision=HIGHEST, preferred_element_type=F32)
        high, low = high_low(matrix)
        mhl[k, :, pl.ds(0, LANES)] = high
        mhl[k, :, pl.ds(LANES, LANES)] = low
        kept = jnp.where((source_slot >= 96) & (source_slot < 112), matrix[48:64], 0.0)
        tw_value = tw_value + pltpu.roll(kept, (16 * k - 96) % LANES, 1)
    tw[...] = tw_value
    halves = [pl.ds(0, 8), pl.ds(8, 8)]

    loads[6].wait()
    loads[7].wait()
    lane64, node64 = iota((64, LANES), 1), iota((64, LANES), 0)
    lane_z = lane64 & 15
    node_c = node64 & 3
    for p in range(2):
        for r in range(2):
            columns = pl.ds(r * LANES, LANES)
            rh[p, :, columns] = rhs_v[p, r]
            own = u_v[p, r].astype(F32)
            z_flag = meta[pl.ds(8 + p * 2 + r, 1), :]
            front = jnp.where(lane_z > 0, pltpu.roll(own, 1, 1), 0.0) * (1.0 - z_flag)
            back = jnp.where(lane_z < 15, pltpu.roll(own, LANES - 1, 1), 0.0) * z_flag
            z_source = jnp.where(node_c == 3, front, jnp.where(node_c == 0, back, 0.0))
            src[p, pl.ds(32, 64), columns] = z_source.astype(BF16)
            src[p, pl.ds(96, 32), columns] = jnp.zeros((32, LANES), BF16)

    for d in (1, 2, zd - 1, zd - 2):
        cls_copies[d].wait_recv()
    pl.semaphore_wait(know.at[0], 2)
    for held in (0, 1, zd - 1, 2, zd - 2):
        for step in far:
            send_cls(held, step)

    for copy in halo_copies:
        copy.wait()

    has_below = jnp.where(gy > 0, 1.0, 0.0)
    has_above = jnp.where(gy < yd - 1, 1.0, 0.0)
    got_below, got_above = halo[0].astype(F32), halo[1].astype(F32)
    for p in range(2):
        for r in range(2):
            y_flag = meta[pl.ds(4 + p * 2 + r, 1), :]
            m_below, m_above = 1.0 - y_flag, y_flag
            if r == 0:
                m_below = m_below * has_below
                other = u_v[p, 1].astype(F32)
            else:
                m_above = m_above * has_above
                other = u_v[p, 0].astype(F32)
            pieces = []
            for a_ in range(4):
                tile_rows = slice(8 * a_, 8 * a_ + 8)
                if r == 0:
                    below = pltpu.roll(got_below[tile_rows], 4, 0) if p == 0 else got_below[tile_rows]
                    above = other[16 * a_ : 16 * a_ + 8]
                else:
                    below = other[16 * a_ + 8 : 16 * a_ + 16]
                    above = got_above[tile_rows] if p == 0 else pltpu.roll(got_above[tile_rows], 4, 0)
                pieces.append(jnp.where(sub8 < 4, above * m_above, below * m_below))
            src[p, pl.ds(0, 32), pl.ds(r * LANES, LANES)] = jnp.concatenate(pieces, axis=0).astype(BF16)

    inv_high_out = ih[:, 48:64, :].reshape(NCLASS * 16, 64)
    inv_low_out = il[:, 48:64, :].reshape(NCLASS * 16, 64)
    lat_out = mhl[:, 48:64, :].reshape(NCLASS * 16, 2 * LANES)

    def class_masks(p, r, rows):
        labels = jnp.broadcast_to(meta[pl.ds(p * 2 + r, 1), :], (rows, LANES))
        return [labels == float(k) for k in range(NCLASS)]

    for p in range(2):
        source = src[p]
        stacked = (
            jnp.dot(lat_out, jnp.concatenate([source, source], axis=0), preferred_element_type=F32)
            + jnp.dot(inv_high_out, rh[p], preferred_element_type=F32)
            + jnp.dot(inv_low_out, rh[p], preferred_element_type=F32)
        )
        for r in range(2):
            wo[p, r] = pick_class(stacked[:, r * LANES : (r + 1) * LANES], 16, class_masks(p, r, 16))

    def class_step(index_row, source_ref):
        base = (jnp.broadcast_to(meta[pl.ds(index_row, 1), :], (8, LANES)) * 16.0).astype(jnp.int32)
        sums = [[], []]
        for m in range(16):
            value = spread(source_ref, m)
            for half in range(2):
                sums[half].append(lanes_of(tw[halves[half], :], base + m) * value)
        return total_of(sums[0]), total_of(sums[1])

    for r in range(2):
        parts = class_step(2 + r, wo.at[0, r])
        for half in range(2):
            ob[0, r, halves[half], :] = parts[half] + wo[1, r, halves[half], :]

    send_own(send_o)

    lane8 = iota((8, LANES), 1)
    pair_first, pair_second = ((lane8 >> 3) & 7) * 16, (lane8 & 7) * 16
    for m in range(16):
        for half in range(2):
            c1s[m, halves[half], :] = lanes_of(tw[halves[half], :], pair_second + m)
            t0s[m, halves[half], :] = lanes_of(tw[halves[half], :], pair_first + m)
    lane16 = iota((16, LANES), 1)

    def pair_product(jj, carry):
        sums = [[], []]
        for m in range(16):
            value = spread(t0s.at[jj], m)
            for half in range(2):
                sums[half].append(c1s[m, halves[half], :] * value)
        product = jnp.concatenate([total_of(sums[0]), total_of(sums[1])], axis=0)
        high = product.astype(BF16)
        rest = product - high.astype(F32)
        middle = rest.astype(BF16)
        low = (rest - middle.astype(F32)).astype(BF16)
        pairs[jj, :, pl.ds(0, LANES)] = jnp.where(lane16 < 64, high.astype(F32), middle.astype(F32)).astype(BF16)
        pairs[jj, :, pl.ds(LANES, LANES)] = jnp.where(lane16 < 64, low.astype(F32), 0.0).astype(BF16)
        return carry

    lax.fori_loop(0, 16, pair_product, 0)

    @pl.when(x < xd - 2)
    def _():
        pl.semaphore_wait(know_x.at[0], 1)

    @pl.when((x > 0) & (x < xd - 2))
    def _():
        pl.semaphore_signal(know_x.at[1], inc=1, device_id=at(dx=-1), device_id_type=MESH)

    @pl.when(x < xd - 3)
    def _():
        pl.semaphore_wait(know_x.at[1], 1)

    def full_planes(p, carry):
        source = src[p]
        both = jnp.concatenate([source, source], axis=0)
        stacked = (
            jnp.dot(mhl[...].reshape(NCLASS * 64, 2 * LANES), both, preferred_element_type=F32)
            + jnp.dot(ih[...].reshape(NCLASS * 64, 64), rh[p], preferred_element_type=F32)
            + jnp.dot(il[...].reshape(NCLASS * 64, 64), rh[p], preferred_element_type=F32)
        )
        for r in range(2):
            labels = jnp.broadcast_to(meta[pl.ds(p * 2 + r, 1), :], (64, LANES))
            out_ref[p, r] = pick_class(stacked[:, r * LANES : (r + 1) * LANES], 64, [labels == float(k) for k in range(NCLASS)])
        return carry

    lax.fori_loop(0, 2, full_planes, 0)

    pair_rows = iota((64, LANES), 0)
    lane_low = lane8 & 15

    def propagators(slots):
        for d in slots:
            hot = []
            for r in range(2):
                labels = lanes_of(jnp.broadcast_to(clsb[d], (8, LANES)), lane_low + 16 * r)
                hot.append((jnp.concatenate([labels] * 8, axis=0).astype(jnp.int32) == pair_rows).astype(F32).astype(BF16))
            one = jnp.concatenate(hot, axis=1)
            every = jnp.dot(pairs[...].reshape(256, 2 * LANES), jnp.concatenate([one, one, one, one], axis=0), preferred_element_type=F32)
            for r in range(2):
                ec[d, r] = every[:, r * LANES : (r + 1) * LANES].reshape(16, 16, LANES)

    propagators((0, 1, 15, 2, 14))
    middle = (7, 3, 13, 5, 11, 4, 12, 6, 10, 9)
    for d in middle:
        cls_copies[d].wait_recv()
        if d == 7:
            send_cls(7, 1)
    for offset in relays:
        relay(o_copies, send_o, offset)
    propagators(middle)
    cls_copies[8].wait_recv()
    propagators((8,))

    def unit_step(i, carry):
        d = lax.rem(z - i + zd, zd)
        for r in range(2):
            sums = [[[] for _ in range(2)] for _ in range(2)]
            for m in range(16):
                values = [spread(up.at[i, r, h], m) for h in range(2)]
                for half in range(2):
                    factor = ec[d, r, m, halves[half], :]
                    for h in range(2):
                        sums[h][half].append(factor * values[h])
            for h in range(2):
                for half in range(2):
                    up[i + 1, r, h, halves[half], :] = total_of(sums[h][half])
        return carry

    for r in range(2):
        for h in range(2):
            up[0, r, h] = (iota((16, LANES), 0) == (lane16 >> 4) + 8 * h).astype(F32)
    lax.fori_loop(0, zd, unit_step, 0)

    px_copies = [
        pltpu.make_async_remote_copy(up.at[zd], px.at[d - 1], px_ss.at[d - 1], px_rs.at[d - 1], device_id=at(dx=d), device_id_type=MESH)
        for d in range(1, xd)
    ]
    for d in range(1, xd):

        @pl.when(x + d < xd)
        def _(d=d):
            px_copies[d - 1].start()


    def expand(value_ref, slot):
        for r in range(2):
            for h in range(2):
                for half in range(2):
                    whole = value_ref[r, h, halves[half], :]
                    for unit in range(8):
                        ex[slot, r, 8 * h + unit, halves[half], :] = lanes_of(whole, lane_low + 16 * unit)

    expand(up.at[z], xd - 1)

    def apply(factors, source):
        sums = [[], []]
        for m in range(16):
            value = spread(source, m)
            for half in range(2):
                sums[half].append(factors[m, halves[half], :] * value)
        return total_of(sums[0]), total_of(sums[1])

    for d in range(1, zd):
        if d not in relays:
            o_copies[d].wait_recv()
    vp[0] = jnp.zeros((2, 16, LANES), F32)

    def group_step(i, carry):
        d = lax.rem(z - i + zd, zd)
        for r in range(2):
            parts = apply(ec.at[d, r], vp.at[i, r])
            for half in range(2):
                vp[i + 1, r, halves[half], :] = parts[half] + ob[d, r, halves[half], :]
        return carry

    lax.fori_loop(0, zd, group_step, 0)
    xo_copies = [
        pltpu.make_async_remote_copy(vp.at[zd], xo.at[d - 1], xo_ss.at[d - 1], xo_rs.at[d - 1], device_id=at(dx=d), device_id_type=MESH)
        for d in range(1, xd)
    ]
    for d in range(1, xd):

        @pl.when(x + d < xd)
        def _(d=d):
            xo_copies[d - 1].start()

    def settle(copies):
        for d in range(1, xd):

            @pl.when(x + d < xd)
            def _(d=d):
                copies[d - 1].wait_send()

            @pl.when(x >= d)
            def _(d=d):
                copies[d - 1].wait_recv()

    settle(px_copies)

    def expand_slot(d, carry):
        expand(px.at[d], d)
        return carry

    lax.fori_loop(0, x, expand_slot, 0)
    xp[0] = inflow_v[...]
    settle(xo_copies)

    def x_step(i, carry):
        d = x - i - 1
        for r in range(2):
            parts = apply(ex.at[d, r], xp.at[i, r])
            for half in range(2):
                xp[i + 1, r, halves[half], :] = parts[half] + xo[d, r, halves[half], :]
        return carry

    lax.fori_loop(0, x, x_step, 0)
    for r in range(2):
        parts = apply(ex.at[xd - 1, r], xp.at[x, r])
        for half in range(2):
            ent[r, halves[half], :] = parts[half] + vp[z, r, halves[half], :]
    for r in range(2):
        parts = class_step(r, ent.at[r])
        for half in range(2):
            tr1[r, halves[half], :] = parts[half] + wo[0, r, halves[half], :]

    for p, trace in enumerate((ent, tr1)):
        high, low = high_low(jnp.concatenate([trace[0], trace[1]], axis=1))
        half_rows = jnp.concatenate([jnp.zeros((96, 2 * LANES), BF16), high, low], axis=0)
        stacked = jnp.dot(mhl[...].reshape(NCLASS * 64, 2 * LANES), jnp.concatenate([half_rows, half_rows], axis=0), preferred_element_type=F32)
        for r in range(2):
            out_ref[p, r] = out_ref[p, r] + pick_class(stacked[:, r * LANES : (r + 1) * LANES], 64, class_masks(p, r, 64))

    for copy in list(cls_copies.values()) + list(o_copies.values()):
        copy.wait_send()


def solution(mesh):
    gxs, yd = mesh.shape["gx"], mesh.shape["gy"]
    zd = min(16, gxs // 2)
    xd = gxs // zd

    def on_device(u_old, rhs, classes, flags, inverse, x_face, lateral_faces, inflow):
        any_space = pl.BlockSpec(memory_space=pl.ANY)
        dma = pltpu.SemaphoreType.DMA
        return pl.pallas_call(
            functools.partial(kernel, xd, zd, yd),
            name="sweep",
            out_shape=pltpu.VMEM((2, 2, 64, LANES), F32),
            in_specs=[any_space] * 8,
            out_specs=pl.BlockSpec(memory_space=pltpu.VMEM),
            scratch_shapes=[
                pltpu.VMEM((2, 2, 64, LANES), BF16),
                pltpu.VMEM((2, 2, 64, LANES), BF16),
                pltpu.VMEM((2, 2, NZ), jnp.int32),
                pltpu.VMEM((2, 2, 2, NZ), jnp.int32),
                pltpu.VMEM((NCLASS, 64, 64), F32),
                pltpu.VMEM((NCLASS, 16, 16), F32),
                pltpu.VMEM((4, NCLASS, 16, 16), F32),
                pltpu.VMEM((2, 16, LANES), F32),
                pltpu.VMEM((2, 32, LANES), BF16),
                pltpu.VMEM((2, 32, LANES), BF16),
                pltpu.VMEM((16, LANES), F32),
                pltpu.VMEM((16, LANES), F32),
                pltpu.VMEM((NCLASS, 64, 64), BF16),
                pltpu.VMEM((NCLASS, 64, 64), BF16),
                pltpu.VMEM((NCLASS, 64, 2 * LANES), BF16),
                pltpu.VMEM((16, LANES), F32),
                pltpu.VMEM((16, 16, LANES), F32),
                pltpu.VMEM((16, 16, LANES), F32),
                pltpu.VMEM((16, 16, 2 * LANES), BF16),
                pltpu.VMEM((2, LANES, 2 * LANES), BF16),
                pltpu.VMEM((2, 64, 2 * LANES), BF16),
                pltpu.VMEM((2, 2, 16, LANES), F32),
                pltpu.VMEM((zd, 1, LANES), F32),
                pltpu.VMEM((zd, 2, 16, LANES), F32),
                pltpu.VMEM((zd, 2, 16, 16, LANES), F32),
                pltpu.VMEM((zd + 1, 2, 2, 16, LANES), F32),
                pltpu.VMEM((zd + 1, 2, 16, LANES), F32),
                pltpu.VMEM((xd - 1, 2, 2, 16, LANES), F32),
                pltpu.VMEM((xd - 1, 2, 16, LANES), F32),
                pltpu.VMEM((xd, 2, 16, 16, LANES), F32),
                pltpu.VMEM((xd, 2, 16, LANES), F32),
                pltpu.VMEM((2, 16, LANES), F32),
                pltpu.VMEM((2, 16, LANES), F32),
                pltpu.SemaphoreType.REGULAR((1,)),
                pltpu.SemaphoreType.REGULAR((2,)),
                dma((8,)),
                dma((2,)),
                dma((2,)),
                dma((zd - 1,)),
                dma((zd - 1,)),
                dma((zd - 1,)),
                dma((zd - 1,)),
                dma((xd - 1,)),
                dma((xd - 1,)),
                dma((xd - 1,)),
                dma((xd - 1,)),
            ],
            compiler_params=pltpu.CompilerParams(collective_id=0, has_side_effects=True),
        )(u_old, rhs, classes, flags, inverse, x_face, lateral_faces, inflow)

    return jax.shard_map(
        on_device,
        mesh=mesh,
        in_specs=(
            P("gx", "gy", None, None),
            P("gx", "gy", None, None),
            P("gx", "gy", None),
            P(None, "gx", "gy", None),
            P(),
            P(),
            P(),
            P("gy", None, None),
        ),
        out_specs=P("gx", "gy", None, None),
        check_vma=False,
    )
```

```python
import functools

import jax
import jax.numpy as jnp
from jax import lax
from jax.experimental import pallas as pl
from jax.experimental.pallas import tpu as pltpu
from jax.sharding import PartitionSpec as P

MESH = pl.DeviceIdType.MESH
NCLASS = 8
NZ = 16
LANES = 128
F32 = jnp.float32
BF16 = jnp.bfloat16
HIGHEST = lax.Precision.HIGHEST


def gather_plan(ring):
    assert ring == 16
    own = (5, -5, 3, -3, 2, -2, 1, -1)
    relays = {5: (2, 1, -1), 11: (-2, -1, 1)}
    covered = {0, 8} | {step % ring for step in own} | {(held + step) % ring for held, steps in relays.items() for step in steps}
    assert covered == set(range(ring)), covered
    return own, relays


def iota(shape, axis):
    return lax.broadcasted_iota(jnp.int32, shape, axis)


def lanes_of(value, index):
    return jnp.take_along_axis(value, index, axis=1, mode="promise_in_bounds")


def spread(ref, row):
    return jnp.broadcast_to(ref[pl.ds(row, 1), :], (8, LANES))


def total_of(terms):
    while len(terms) > 1:
        terms = [sum(terms[i : i + 2]) for i in range(0, len(terms), 2)]
    return terms[0]


def high_low(value):
    high = value.astype(BF16)
    return high, (value - high.astype(F32)).astype(BF16)


def pick_class(stacked, rows, masks):
    result = stacked[0:rows]
    for k in range(1, NCLASS):
        result = jnp.where(masks[k], stacked[k * rows : (k + 1) * rows], result)
    return result


def kernel(
    xd, zd, yd,
    u_hbm, rhs_hbm, cls_hbm, flg_hbm, inv_hbm, xf_hbm, lat_hbm, inflow_hbm,
    out_ref,
    u_v, rhs_v, cls_v, flg_v, inv_v, xf_v, lat_v, inflow_v, border, halo,
    meta_in, meta, ih, il, mhl, tw, c1s, t0s, pairs, src, rh, wo,
    clsb, ob, ec, up, vp, px, xo, ex, xp, ent, tr1,
    know, know_x, local_sem, halo_ss, halo_rs, cls_ss, cls_rs, o_ss, o_rs, px_ss, px_rs, xo_ss, xo_rs,
):
    gx, gy = lax.axis_index("gx"), lax.axis_index("gy")
    x, z = gx // zd, lax.rem(gx, zd)

    def at(dx=0, dz=0, dy=0):
        gx_to = lax.rem(x + dx + xd, xd) * zd + lax.rem(z + dz + zd, zd)
        return (gx_to, lax.rem(gy + dy + yd, yd))

    loads = [
        pltpu.make_async_copy(a, b, local_sem.at[i])
        for i, (a, b) in enumerate(
            [(cls_hbm, cls_v), (flg_hbm, flg_v), (u_hbm, u_v), (inv_hbm, inv_v), (lat_hbm, lat_v), (xf_hbm, xf_v), (rhs_hbm, rhs_v), (inflow_hbm, inflow_v)]
        )
    ]
    for load in loads:
        load.start()
    own_steps, relays = gather_plan(zd)
    barrier = pltpu.get_barrier_semaphore()
    for peer in (at(dy=1), at(dy=-1)) + tuple(at(dz=d) for d in (1, -1, 2, -2, 3, -3)):
        pl.semaphore_signal(barrier, inc=1, device_id=peer, device_id_type=MESH)

    @pl.when(x > 0)
    def _():
        pl.semaphore_signal(barrier, inc=1, device_id=at(dx=-1), device_id_type=MESH)

    @pl.when(x < xd - 1)
    def _():
        pl.semaphore_signal(barrier, inc=1, device_id=at(dx=1), device_id_type=MESH)

    greeted = 8 + jnp.where(x > 0, 1, 0) + jnp.where(x < xd - 1, 1, 0)

    def settle(semaphore, ref):
        pltpu.make_async_copy(ref, ref, semaphore).wait()

    def tell(semaphore, step):
        for sign in (1, -1):
            pl.semaphore_signal(semaphore, inc=1, device_id=at(dz=sign * step), device_id_type=MESH)

    meta_in[...] = jnp.zeros_like(meta_in)
    loads[0].wait()
    loads[1].wait()
    for p in range(2):
        for r in range(2):
            meta_in[pl.ds(p * 2 + r, 1), pl.ds(0, NZ)] = cls_v[p, pl.ds(r, 1), :].astype(F32)
            for f in range(2):
                meta_in[pl.ds(4 + f * 4 + p * 2 + r, 1), pl.ds(0, NZ)] = flg_v[f, p, pl.ds(r, 1), :].astype(F32)
    row, col = iota((LANES, LANES), 0), iota((LANES, LANES), 1)
    tile = ((row < NZ) & (row == (col & 15))).astype(BF16)
    meta_value = jnp.dot(meta_in[...].astype(BF16), tile, preferred_element_type=F32)
    meta[...] = meta_value
    pair = meta_value[0:2] * 8.0 + meta_value[2:4]
    clsb[0] = jnp.where(iota((1, LANES), 1) < NZ, pair[0:1], pair[1:2])

    loads[2].wait()
    sub8 = iota((8, LANES), 0)
    top = [u_v[p, 1].astype(F32) for p in range(2)]
    bottom = [u_v[p, 0].astype(F32) for p in range(2)]
    packed_top, packed_bottom = [], []
    for a_ in range(4):
        low_rows, high_rows = slice(16 * a_, 16 * a_ + 8), slice(16 * a_ + 8, 16 * a_ + 16)
        packed_top.append(jnp.where(sub8 < 4, pltpu.roll(top[0][high_rows], 4, 0), top[1][high_rows]))
        packed_bottom.append(jnp.where(sub8 < 4, bottom[0][low_rows], pltpu.roll(bottom[1][low_rows], 4, 0)))
    border[0] = jnp.concatenate(packed_top, axis=0).astype(BF16)
    border[1] = jnp.concatenate(packed_bottom, axis=0).astype(BF16)
    pl.semaphore_wait(barrier, greeted)

    tell(know.at[0], 2)

    halo_copies = [
        pltpu.make_async_remote_copy(border.at[0], halo.at[0], halo_ss, halo_rs, device_id=at(dy=1), device_id_type=MESH),
        pltpu.make_async_remote_copy(border.at[1], halo.at[1], halo_ss, halo_rs, device_id=at(dy=-1), device_id_type=MESH),
    ]
    for copy in halo_copies:
        copy.start()
    @pl.when((x > 0) & (x < xd - 1))
    def _():
        pl.semaphore_signal(know_x.at[0], inc=1, device_id=at(dx=-1), device_id_type=MESH)

    near_steps = (3, 2, -2, 1, -1)
    filled = {"cls": [], "o": []}

    def send_cls(held, step):
        to = (held + step) % zd
        assert to not in filled["cls"]
        filled["cls"].append(to)
        arrival = cls_rs.at[0 if held == 0 and step in near_steps else 1]
        pltpu.make_async_remote_copy(clsb.at[held], clsb.at[to], cls_ss, arrival, device_id=at(dz=step), device_id_type=MESH).start()

    def send_o(held, step):
        to = (held + step) % zd
        assert to not in filled["o"]
        filled["o"].append(to)
        arrival = o_rs.at[0 if to == 5 else 1 if to == 11 else 2]
        pltpu.make_async_remote_copy(ob.at[held], ob.at[to], o_ss, arrival, device_id=at(dz=step), device_id_type=MESH).start()

    for step in near_steps:
        send_cls(0, step)
    halves_of_8 = [
        pltpu.make_async_remote_copy(ob.at[held, r], ob.at[8, r], o_ss, o_rs.at[2], device_id=at(dz=step), device_id_type=MESH)
        for r, (held, step) in enumerate([(5, 3), (11, -3)])
    ]

    loads[3].wait()
    loads[4].wait()
    loads[5].wait()
    inv_all = inv_v[...].reshape(NCLASS * 64, 64)
    ih_value, il_value = high_low(inv_all)
    ih[...] = ih_value.reshape(NCLASS, 64, 64)
    il[...] = il_value.reshape(NCLASS, 64, 64)
    node, slot = iota((64, LANES), 0), iota((64, LANES), 1)
    face, j = slot >> 4, slot & 15
    a, b = j >> 2, j & 3
    y_node = 16 * a + b
    wanted = jnp.where(face == 0, y_node, jnp.where(face == 1, y_node + 12, jnp.where(face == 2, 4 * j, jnp.where(face == 3, 4 * j + 3, jnp.where(face == 4, j, -1)))))
    faces_of = jnp.dot(inv_all, (node == wanted).astype(F32), precision=HIGHEST, preferred_element_type=F32)
    tables = jnp.concatenate([lat_v[...].reshape(4 * NCLASS * 16, 16), xf_v[...].reshape(NCLASS * 16, 16)], axis=0)
    source_slot, sj = iota((16, LANES), 1), iota((16, LANES), 0)

    def slot_face_and_j(s):
        y_face = jnp.where((s & 7) < 4, 1, 0)
        y_j = 4 * (s >> 3) + (s & 3)
        t = s - 32
        z_face = jnp.where((t & 3) == 3, 2, jnp.where((t & 3) == 0, 3, -1))
        z_j = t >> 2
        in_face = jnp.where(s < 32, y_face, jnp.where(s < 96, z_face, 4))
        in_j = jnp.where(s < 32, y_j, jnp.where(s < 96, z_j, s & 15))
        return in_face, in_j

    slot_face, column_j = slot_face_and_j(source_slot)
    placed = jnp.dot(tables, (column_j == sj).astype(F32), precision=HIGHEST, preferred_element_type=F32)
    tw_value = jnp.zeros((16, LANES), F32)
    for k in range(NCLASS):
        blocks = []
        for f in range(5):
            start = (f * NCLASS + k) * 16
            blocks.append(jnp.where(slot_face == f, placed[start : start + 16], 0.0))
        blocks.append(jnp.zeros((48, LANES), F32))
        matrix = -jnp.dot(faces_of[k * 64 : (k + 1) * 64], jnp.concatenate(blocks, axis=0), precision=HIGHEST, preferred_element_type=F32)
        high, low = high_low(matrix)
        mhl[k, :, pl.ds(0, LANES)] = high
        mhl[k, :, pl.ds(LANES, LANES)] = low
        kept = jnp.where((source_slot >= 96) & (source_slot < 112), matrix[48:64], 0.0)
        tw_value = tw_value + pltpu.roll(kept, (16 * k - 96) % LANES, 1)
    tw[...] = tw_value
    halves = [pl.ds(0, 8), pl.ds(8, 8)]

    loads[6].wait()
    loads[7].wait()
    lane64, node64 = iota((64, LANES), 1), iota((64, LANES), 0)
    lane_z = lane64 & 15
    node_c = node64 & 3
    for p in range(2):
        for r in range(2):
            columns = pl.ds(r * LANES, LANES)
            rh[p, :, columns] = rhs_v[p, r]
            own = u_v[p, r].astype(F32)
            z_flag = meta[pl.ds(8 + p * 2 + r, 1), :]
            front = jnp.where(lane_z > 0, pltpu.roll(own, 1, 1), 0.0) * (1.0 - z_flag)
            back = jnp.where(lane_z < 15, pltpu.roll(own, LANES - 1, 1), 0.0) * z_flag
            z_source = jnp.where(node_c == 3, front, jnp.where(node_c == 0, back, 0.0))
            src[p, pl.ds(32, 64), columns] = z_source.astype(BF16)
            src[p, pl.ds(96, 32), columns] = jnp.zeros((32, LANES), BF16)

    settle(halo_rs, halo)

    @pl.when(x < xd - 2)
    def _():
        pl.semaphore_wait(know_x.at[0], 1)

    @pl.when((x > 0) & (x < xd - 2))
    def _():
        pl.semaphore_signal(know_x.at[1], inc=1, device_id=at(dx=-1), device_id_type=MESH)

    has_below = jnp.where(gy > 0, 1.0, 0.0)
    has_above = jnp.where(gy < yd - 1, 1.0, 0.0)
    got_below, got_above = halo[0].astype(F32), halo[1].astype(F32)
    for p in range(2):
        for r in range(2):
            y_flag = meta[pl.ds(4 + p * 2 + r, 1), :]
            m_below, m_above = 1.0 - y_flag, y_flag
            if r == 0:
                m_below = m_below * has_below
                other = u_v[p, 1].astype(F32)
            else:
                m_above = m_above * has_above
                other = u_v[p, 0].astype(F32)
            pieces = []
            for a_ in range(4):
                tile_rows = slice(8 * a_, 8 * a_ + 8)
                if r == 0:
                    below = pltpu.roll(got_below[tile_rows], 4, 0) if p == 0 else got_below[tile_rows]
                    above = other[16 * a_ : 16 * a_ + 8]
                else:
                    below = other[16 * a_ + 8 : 16 * a_ + 16]
                    above = got_above[tile_rows] if p == 0 else pltpu.roll(got_above[tile_rows], 4, 0)
                pieces.append(jnp.where(sub8 < 4, above * m_above, below * m_below))
            src[p, pl.ds(0, 32), pl.ds(r * LANES, LANES)] = jnp.concatenate(pieces, axis=0).astype(BF16)

    inv_high_out = ih[:, 48:64, :].reshape(NCLASS * 16, 64)
    inv_low_out = il[:, 48:64, :].reshape(NCLASS * 16, 64)
    lat_out = mhl[:, 48:64, :].reshape(NCLASS * 16, 2 * LANES)

    def class_masks(p, r, rows):
        labels = jnp.broadcast_to(meta[pl.ds(p * 2 + r, 1), :], (rows, LANES))
        return [labels == float(k) for k in range(NCLASS)]

    for p in range(2):
        source = src[p]
        stacked = (
            jnp.dot(lat_out, jnp.concatenate([source, source], axis=0), preferred_element_type=F32)
            + jnp.dot(inv_high_out, rh[p], preferred_element_type=F32)
            + jnp.dot(inv_low_out, rh[p], preferred_element_type=F32)
        )
        for r in range(2):
            wo[p, r] = pick_class(stacked[:, r * LANES : (r + 1) * LANES], 16, class_masks(p, r, 16))

    def class_step(index_row, source_ref):
        base = (jnp.broadcast_to(meta[pl.ds(index_row, 1), :], (8, LANES)) * 16.0).astype(jnp.int32)
        sums = [[], []]
        for m in range(16):
            value = spread(source_ref, m)
            for half in range(2):
                sums[half].append(lanes_of(tw[halves[half], :], base + m) * value)
        return total_of(sums[0]), total_of(sums[1])

    for r in range(2):
        parts = class_step(2 + r, wo.at[0, r])
        for half in range(2):
            ob[0, r, halves[half], :] = parts[half] + wo[1, r, halves[half], :]

    pl.semaphore_wait(know.at[0], 2)
    for step in own_steps[:2]:
        send_o(0, step)
    for step in (5, -5):
        send_cls(0, step)

    lane8 = iota((8, LANES), 1)
    pair_first, pair_second = ((lane8 >> 3) & 7) * 16, (lane8 & 7) * 16
    for m in range(16):
        for half in range(2):
            c1s[m, halves[half], :] = lanes_of(tw[halves[half], :], pair_second + m)
            t0s[m, halves[half], :] = lanes_of(tw[halves[half], :], pair_first + m)
    lane16 = iota((16, LANES), 1)

    def pair_product(jj, carry):
        sums = [[], []]
        for m in range(16):
            value = spread(t0s.at[jj], m)
            for half in range(2):
                sums[half].append(c1s[m, halves[half], :] * value)
        product = jnp.concatenate([total_of(sums[0]), total_of(sums[1])], axis=0)
        high = product.astype(BF16)
        rest = product - high.astype(F32)
        middle = rest.astype(BF16)
        low = (rest - middle.astype(F32)).astype(BF16)
        pairs[jj, :, pl.ds(0, LANES)] = jnp.where(lane16 < 64, high.astype(F32), middle.astype(F32)).astype(BF16)
        pairs[jj, :, pl.ds(LANES, LANES)] = jnp.where(lane16 < 64, low.astype(F32), 0.0).astype(BF16)
        return carry

    lax.fori_loop(0, 16, pair_product, 0)

    settle(cls_rs.at[0], clsb.at[pl.ds(0, 5)])
    for held in (2, zd - 2, 1, zd - 1):
        for step in (5, -5):
            if (held + step) % zd not in filled["cls"]:
                send_cls(held, step)
    send_cls(3, 5)
    def full_planes(p, carry):
        source = src[p]
        both = jnp.concatenate([source, source], axis=0)
        stacked = (
            jnp.dot(mhl[...].reshape(NCLASS * 64, 2 * LANES), both, preferred_element_type=F32)
            + jnp.dot(ih[...].reshape(NCLASS * 64, 64), rh[p], preferred_element_type=F32)
            + jnp.dot(il[...].reshape(NCLASS * 64, 64), rh[p], preferred_element_type=F32)
        )
        for r in range(2):
            labels = jnp.broadcast_to(meta[pl.ds(p * 2 + r, 1), :], (64, LANES))
            out_ref[p, r] = pick_class(stacked[:, r * LANES : (r + 1) * LANES], 64, [labels == float(k) for k in range(NCLASS)])
        return carry

    lax.fori_loop(0, 2, full_planes, 0)

    pair_rows = iota((64, LANES), 0)
    lane_low = lane8 & 15

    def propagators(slots):
        for d in slots:
            hot = []
            for r in range(2):
                labels = lanes_of(jnp.broadcast_to(clsb[d], (8, LANES)), lane_low + 16 * r)
                hot.append((jnp.concatenate([labels] * 8, axis=0).astype(jnp.int32) == pair_rows).astype(F32).astype(BF16))
            one = jnp.concatenate(hot, axis=1)
            every = jnp.dot(pairs[...].reshape(256, 2 * LANES), jnp.concatenate([one, one, one, one], axis=0), preferred_element_type=F32)
            for r in range(2):
                ec[d, r] = every[:, r * LANES : (r + 1) * LANES].reshape(16, 16, LANES)

    for step in own_steps[2:]:
        send_o(0, step)
    assert len(filled["cls"]) == zd - 1
    propagators((0, 1, 15, 2, 14))
    for r, (held, steps) in enumerate(relays.items()):
        settle(o_rs.at[r], ob.at[held])
        halves_of_8[r].start()
        for step in steps:
            send_o(held, step)
    middle = (3, 5, 11, 4, 12, 6, 10, 7, 9, 13, 8)
    settle(cls_rs.at[1], clsb.at[pl.ds(0, zd - 6)])
    propagators(middle)

    def unit_step(i, carry):
        d = lax.rem(z - i + zd, zd)
        for r in range(2):
            sums = [[[] for _ in range(2)] for _ in range(2)]
            for m in range(16):
                values = [spread(up.at[i, r, h], m) for h in range(2)]
                for half in range(2):
                    factor = ec[d, r, m, halves[half], :]
                    for h in range(2):
                        sums[h][half].append(factor * values[h])
            for h in range(2):
                for half in range(2):
                    up[i + 1, r, h, halves[half], :] = total_of(sums[h][half])
        return carry

    for r in range(2):
        for h in range(2):
            up[0, r, h] = (iota((16, LANES), 0) == (lane16 >> 4) + 8 * h).astype(F32)
    lax.fori_loop(0, zd, unit_step, 0)

    @pl.when(x < xd - 3)
    def _():
        pl.semaphore_wait(know_x.at[1], 1)

    px_copies = [
        pltpu.make_async_remote_copy(up.at[zd], px.at[d - 1], px_ss, px_rs, device_id=at(dx=d), device_id_type=MESH)
        for d in range(1, xd)
    ]
    for d in range(1, xd):

        @pl.when(x + d < xd)
        def _(d=d):
            px_copies[d - 1].start()


    def expand(value_ref, slot):
        for r in range(2):
            for h in range(2):
                for half in range(2):
                    whole = value_ref[r, h, halves[half], :]
                    for unit in range(8):
                        ex[slot, r, 8 * h + unit, halves[half], :] = lanes_of(whole, lane_low + 16 * unit)

    expand(up.at[z], xd - 1)

    def apply(factors, source):
        sums = [[], []]
        for m in range(16):
            value = spread(source, m)
            for half in range(2):
                sums[half].append(factors[m, halves[half], :] * value)
        return total_of(sums[0]), total_of(sums[1])

    assert len(filled["o"]) == zd - 2
    settle(o_rs.at[2], ob.at[pl.ds(0, zd - 3)])
    vp[0] = jnp.zeros((2, 16, LANES), F32)

    def group_step(i, carry):
        d = lax.rem(z - i + zd, zd)
        for r in range(2):
            parts = apply(ec.at[d, r], vp.at[i, r])
            for half in range(2):
                vp[i + 1, r, halves[half], :] = parts[half] + ob[d, r, halves[half], :]
        return carry

    lax.fori_loop(0, zd, group_step, 0)
    xo_copies = [
        pltpu.make_async_remote_copy(vp.at[zd], xo.at[d - 1], xo_ss, xo_rs, device_id=at(dx=d), device_id_type=MESH)
        for d in range(1, xd)
    ]
    for d in range(1, xd):

        @pl.when(x + d < xd)
        def _(d=d):
            xo_copies[d - 1].start()

    def settle_x(send_sem, recv_sem, ref):
        for n in range(1, xd):

            @pl.when(x == xd - 1 - n)
            def _(n=n):
                settle(send_sem, ref.at[pl.ds(0, n)])

            @pl.when(x == n)
            def _(n=n):
                settle(recv_sem, ref.at[pl.ds(0, n)])

    settle_x(px_ss, px_rs, px)

    def expand_slot(d, carry):
        expand(px.at[d], d)
        return carry

    lax.fori_loop(0, x, expand_slot, 0)
    xp[0] = inflow_v[...]
    settle_x(xo_ss, xo_rs, xo)

    def x_step(i, carry):
        d = x - i - 1
        for r in range(2):
            parts = apply(ex.at[d, r], xp.at[i, r])
            for half in range(2):
                xp[i + 1, r, halves[half], :] = parts[half] + xo[d, r, halves[half], :]
        return carry

    lax.fori_loop(0, x, x_step, 0)
    for r in range(2):
        parts = apply(ex.at[xd - 1, r], xp.at[x, r])
        for half in range(2):
            ent[r, halves[half], :] = parts[half] + vp[z, r, halves[half], :]
    for r in range(2):
        parts = class_step(r, ent.at[r])
        for half in range(2):
            tr1[r, halves[half], :] = parts[half] + wo[0, r, halves[half], :]

    for p, trace in enumerate((ent, tr1)):
        high, low = high_low(jnp.concatenate([trace[0], trace[1]], axis=1))
        half_rows = jnp.concatenate([jnp.zeros((96, 2 * LANES), BF16), high, low], axis=0)
        stacked = jnp.dot(mhl[...].reshape(NCLASS * 64, 2 * LANES), jnp.concatenate([half_rows, half_rows], axis=0), preferred_element_type=F32)
        for r in range(2):
            out_ref[p, r] = out_ref[p, r] + pick_class(stacked[:, r * LANES : (r + 1) * LANES], 64, class_masks(p, r, 64))

    settle(halo_ss, halo)
    settle(cls_ss, clsb.at[pl.ds(0, zd - 1)])
    settle(o_ss, ob.at[pl.ds(0, zd - 1)])


def solution(mesh):
    gxs, yd = mesh.shape["gx"], mesh.shape["gy"]
    zd = min(16, gxs // 2)
    xd = gxs // zd

    def on_device(u_old, rhs, classes, flags, inverse, x_face, lateral_faces, inflow):
        any_space = pl.BlockSpec(memory_space=pl.ANY)
        dma = pltpu.SemaphoreType.DMA
        return pl.pallas_call(
            functools.partial(kernel, xd, zd, yd),
            name="sweep",
            out_shape=pltpu.VMEM((2, 2, 64, LANES), F32),
            in_specs=[any_space] * 8,
            out_specs=pl.BlockSpec(memory_space=pltpu.VMEM),
            scratch_shapes=[
                pltpu.VMEM((2, 2, 64, LANES), BF16),
                pltpu.VMEM((2, 2, 64, LANES), BF16),
                pltpu.VMEM((2, 2, NZ), jnp.int32),
                pltpu.VMEM((2, 2, 2, NZ), jnp.int32),
                pltpu.VMEM((NCLASS, 64, 64), F32),
                pltpu.VMEM((NCLASS, 16, 16), F32),
                pltpu.VMEM((4, NCLASS, 16, 16), F32),
                pltpu.VMEM((2, 16, LANES), F32),
                pltpu.VMEM((2, 32, LANES), BF16),
                pltpu.VMEM((2, 32, LANES), BF16),
                pltpu.VMEM((16, LANES), F32),
                pltpu.VMEM((16, LANES), F32),
                pltpu.VMEM((NCLASS, 64, 64), BF16),
                pltpu.VMEM((NCLASS, 64, 64), BF16),
                pltpu.VMEM((NCLASS, 64, 2 * LANES), BF16),
                pltpu.VMEM((16, LANES), F32),
                pltpu.VMEM((16, 16, LANES), F32),
                pltpu.VMEM((16, 16, LANES), F32),
                pltpu.VMEM((16, 16, 2 * LANES), BF16),
                pltpu.VMEM((2, LANES, 2 * LANES), BF16),
                pltpu.VMEM((2, 64, 2 * LANES), BF16),
                pltpu.VMEM((2, 2, 16, LANES), F32),
                pltpu.VMEM((zd, 1, LANES), F32),
                pltpu.VMEM((zd, 2, 16, LANES), F32),
                pltpu.VMEM((zd, 2, 16, 16, LANES), F32),
                pltpu.VMEM((zd + 1, 2, 2, 16, LANES), F32),
                pltpu.VMEM((zd + 1, 2, 16, LANES), F32),
                pltpu.VMEM((xd - 1, 2, 2, 16, LANES), F32),
                pltpu.VMEM((xd - 1, 2, 16, LANES), F32),
                pltpu.VMEM((xd, 2, 16, 16, LANES), F32),
                pltpu.VMEM((xd, 2, 16, LANES), F32),
                pltpu.VMEM((2, 16, LANES), F32),
                pltpu.VMEM((2, 16, LANES), F32),
                pltpu.SemaphoreType.REGULAR((1,)),
                pltpu.SemaphoreType.REGULAR((2,)),
                dma((8,)),
                dma,
                dma,
                dma,
                dma((2,)),
                dma,
                dma((3,)),
                dma,
                dma,
                dma,
                dma,
            ],
            compiler_params=pltpu.CompilerParams(collective_id=0, has_side_effects=True),
        )(u_old, rhs, classes, flags, inverse, x_face, lateral_faces, inflow)

    return jax.shard_map(
        on_device,
        mesh=mesh,
        in_specs=(
            P("gx", "gy", None, None),
            P("gx", "gy", None, None),
            P("gx", "gy", None),
            P(None, "gx", "gy", None),
            P(),
            P(),
            P(),
            P("gy", None, None),
        ),
        out_specs=P("gx", "gy", None, None),
        check_vma=False,
    )
```

```python
import functools

import jax
import jax.numpy as jnp
from jax import lax
from jax.experimental import pallas as pl
from jax.experimental.pallas import tpu as pltpu
from jax.sharding import PartitionSpec as P

MESH = pl.DeviceIdType.MESH
NCLASS = 8
NZ = 16
LANES = 128
F32 = jnp.float32
BF16 = jnp.bfloat16
HIGHEST = lax.Precision.HIGHEST


def gather_plan(ring):
    assert ring == 16
    own = (5, -5, 3, -3, 2, -2, 1, -1)
    relays = {5: (2, 1, -1), 11: (-2, -1, 1)}
    covered = {0, 8} | {step % ring for step in own} | {(held + step) % ring for held, steps in relays.items() for step in steps}
    assert covered == set(range(ring)), covered
    return own, relays


def iota(shape, axis):
    return lax.broadcasted_iota(jnp.int32, shape, axis)


def lanes_of(value, index):
    return jnp.take_along_axis(value, index, axis=1, mode="promise_in_bounds")


def spread(ref, row):
    return jnp.broadcast_to(ref[pl.ds(row, 1), :], (8, LANES))


def total_of(terms):
    while len(terms) > 1:
        terms = [sum(terms[i : i + 2]) for i in range(0, len(terms), 2)]
    return terms[0]


def high_low(value):
    high = value.astype(BF16)
    return high, (value - high.astype(F32)).astype(BF16)


def pick_class(stacked, rows, masks):
    result = stacked[0:rows]
    for k in range(1, NCLASS):
        result = jnp.where(masks[k], stacked[k * rows : (k + 1) * rows], result)
    return result


def kernel(
    xd, zd, yd,
    u_hbm, rhs_hbm, cls_hbm, flg_hbm, inv_hbm, xf_hbm, lat_hbm, inflow_hbm,
    out_ref,
    u_v, rhs_v, cls_v, flg_v, inv_v, xf_v, lat_v, inflow_v, border, halo,
    meta_in, meta, ih, il, mhl, tw, c1s, t0s, pairs, src, rh, wo,
    clsb, ob, ec, up, vp, px, xo, ex, xp, ent, tr1,
    know, know_x, local_sem, halo_ss, halo_rs, cls_ss, cls_rs, o_ss, o_rs, px_ss, px_rs, xo_ss, xo_rs,
):
    gx, gy = lax.axis_index("gx"), lax.axis_index("gy")
    x, z = gx // zd, lax.rem(gx, zd)

    def at(dx=0, dz=0, dy=0):
        gx_to = lax.rem(x + dx + xd, xd) * zd + lax.rem(z + dz + zd, zd)
        return (gx_to, lax.rem(gy + dy + yd, yd))

    own_steps, relays = gather_plan(zd)
    barrier = pltpu.get_barrier_semaphore()
    for d in (3, -3, 2, -2, 1, -1):
        pl.semaphore_signal(barrier, inc=1, device_id=at(dz=d), device_id_type=MESH)
    has_below, has_above = gy > 0, gy < yd - 1

    @pl.when(has_above)
    def _():
        pl.semaphore_signal(barrier, inc=1, device_id=at(dy=1), device_id_type=MESH)

    @pl.when(has_below)
    def _():
        pl.semaphore_signal(barrier, inc=1, device_id=at(dy=-1), device_id_type=MESH)

    @pl.when(x > 0)
    def _():
        pl.semaphore_signal(barrier, inc=1, device_id=at(dx=-1), device_id_type=MESH)

    @pl.when(x < xd - 1)
    def _():
        pl.semaphore_signal(barrier, inc=1, device_id=at(dx=1), device_id_type=MESH)

    greeted = 6 + sum(jnp.where(there, 1, 0) for there in (has_below, has_above, x > 0, x < xd - 1))
    loads = [
        pltpu.make_async_copy(a, b, local_sem.at[i])
        for i, (a, b) in enumerate(
            [(cls_hbm, cls_v), (flg_hbm, flg_v), (u_hbm, u_v), (inv_hbm, inv_v), (lat_hbm, lat_v), (xf_hbm, xf_v), (rhs_hbm, rhs_v), (inflow_hbm, inflow_v)]
        )
    ]
    for load in loads:
        load.start()

    def settle(semaphore, ref):
        pltpu.make_async_copy(ref, ref, semaphore).wait()

    def tell(semaphore, step):
        for sign in (1, -1):
            pl.semaphore_signal(semaphore, inc=1, device_id=at(dz=sign * step), device_id_type=MESH)

    meta_in[...] = jnp.zeros_like(meta_in)
    loads[0].wait()
    loads[1].wait()
    for p in range(2):
        for r in range(2):
            meta_in[pl.ds(p * 2 + r, 1), pl.ds(0, NZ)] = cls_v[p, pl.ds(r, 1), :].astype(F32)
            for f in range(2):
                meta_in[pl.ds(4 + f * 4 + p * 2 + r, 1), pl.ds(0, NZ)] = flg_v[f, p, pl.ds(r, 1), :].astype(F32)
    row, col = iota((LANES, LANES), 0), iota((LANES, LANES), 1)
    tile = ((row < NZ) & (row == (col & 15))).astype(BF16)
    meta_value = jnp.dot(meta_in[...].astype(BF16), tile, preferred_element_type=F32)
    meta[...] = meta_value
    pair = meta_value[0:2] * 8.0 + meta_value[2:4]
    clsb[0] = jnp.where(iota((1, LANES), 1) < NZ, pair[0:1], pair[1:2])

    loads[2].wait()
    sub8 = iota((8, LANES), 0)
    top = [u_v[p, 1].astype(F32) for p in range(2)]
    bottom = [u_v[p, 0].astype(F32) for p in range(2)]
    packed_top, packed_bottom = [], []
    for a_ in range(4):
        low_rows, high_rows = slice(16 * a_, 16 * a_ + 8), slice(16 * a_ + 8, 16 * a_ + 16)
        packed_top.append(jnp.where(sub8 < 4, pltpu.roll(top[0][high_rows], 4, 0), top[1][high_rows]))
        packed_bottom.append(jnp.where(sub8 < 4, bottom[0][low_rows], pltpu.roll(bottom[1][low_rows], 4, 0)))
    border[0] = jnp.concatenate(packed_top, axis=0).astype(BF16)
    border[1] = jnp.concatenate(packed_bottom, axis=0).astype(BF16)
    pl.semaphore_wait(barrier, greeted)

    tell(know.at[0], 2)

    halo_copies = [
        pltpu.make_async_remote_copy(border.at[0], halo.at[0], halo_ss, halo_rs, device_id=at(dy=1), device_id_type=MESH),
        pltpu.make_async_remote_copy(border.at[1], halo.at[1], halo_ss, halo_rs, device_id=at(dy=-1), device_id_type=MESH),
    ]
    @pl.when(has_above)
    def _():
        halo_copies[0].start()

    @pl.when(has_below)
    def _():
        halo_copies[1].start()

    @pl.when(gy == 0)
    def _():
        halo[0] = jnp.zeros((32, LANES), BF16)

    @pl.when(gy == yd - 1)
    def _():
        halo[1] = jnp.zeros((32, LANES), BF16)

    @pl.when((x > 0) & (x < xd - 1))
    def _():
        pl.semaphore_signal(know_x.at[0], inc=1, device_id=at(dx=-1), device_id_type=MESH)

    near_steps = (2, -2, 3, 1, -1)
    filled = {"cls": [], "o": []}

    def send_cls(held, step):
        to = (held + step) % zd
        assert to not in filled["cls"]
        filled["cls"].append(to)
        arrival = cls_rs.at[{3: 2, 8: 3}.get(to, 0 if held == 0 and step in near_steps else 1)]
        pltpu.make_async_remote_copy(clsb.at[held], clsb.at[to], cls_ss, arrival, device_id=at(dz=step), device_id_type=MESH).start()

    def send_o(held, step):
        to = (held + step) % zd
        assert to not in filled["o"]
        filled["o"].append(to)
        arrival = o_rs.at[0 if to == 5 else 1 if to == 11 else 2]
        pltpu.make_async_remote_copy(ob.at[held], ob.at[to], o_ss, arrival, device_id=at(dz=step), device_id_type=MESH).start()

    for step in near_steps:
        send_cls(0, step)
    halves_of_8 = [
        pltpu.make_async_remote_copy(ob.at[held, r], ob.at[8, r], o_ss, o_rs.at[2], device_id=at(dz=step), device_id_type=MESH)
        for r, (held, step) in enumerate([(5, 3), (11, -3)])
    ]

    loads[3].wait()
    loads[4].wait()
    loads[5].wait()
    inv_all = inv_v[...].reshape(NCLASS * 64, 64)
    ih_value, il_value = high_low(inv_all)
    ih[...] = ih_value.reshape(NCLASS, 64, 64)
    il[...] = il_value.reshape(NCLASS, 64, 64)
    node, slot = iota((64, LANES), 0), iota((64, LANES), 1)
    face, j = slot >> 4, slot & 15
    a, b = j >> 2, j & 3
    y_node = 16 * a + b
    wanted = jnp.where(face == 0, y_node, jnp.where(face == 1, y_node + 12, jnp.where(face == 2, 4 * j, jnp.where(face == 3, 4 * j + 3, jnp.where(face == 4, j, -1)))))
    faces_of = jnp.dot(inv_all, (node == wanted).astype(F32), precision=HIGHEST, preferred_element_type=F32)
    tables = jnp.concatenate([lat_v[...].reshape(4 * NCLASS * 16, 16), xf_v[...].reshape(NCLASS * 16, 16)], axis=0)
    source_slot, sj = iota((16, LANES), 1), iota((16, LANES), 0)

    def slot_face_and_j(s):
        y_face = jnp.where((s & 7) < 4, 1, 0)
        y_j = 4 * (s >> 3) + (s & 3)
        t = s - 32
        z_face = jnp.where((t & 3) == 3, 2, jnp.where((t & 3) == 0, 3, -1))
        z_j = t >> 2
        in_face = jnp.where(s < 32, y_face, jnp.where(s < 96, z_face, 4))
        in_j = jnp.where(s < 32, y_j, jnp.where(s < 96, z_j, s & 15))
        return in_face, in_j

    slot_face, column_j = slot_face_and_j(source_slot)
    placed = jnp.dot(tables, (column_j == sj).astype(F32), precision=HIGHEST, preferred_element_type=F32)
    tw_value = jnp.zeros((16, LANES), F32)
    for k in range(NCLASS):
        blocks = []
        for f in range(5):
            start = (f * NCLASS + k) * 16
            blocks.append(jnp.where(slot_face == f, placed[start : start + 16], 0.0))
        blocks.append(jnp.zeros((48, LANES), F32))
        matrix = -jnp.dot(faces_of[k * 64 : (k + 1) * 64], jnp.concatenate(blocks, axis=0), precision=HIGHEST, preferred_element_type=F32)
        high, low = high_low(matrix)
        mhl[k, :, pl.ds(0, LANES)] = high
        mhl[k, :, pl.ds(LANES, LANES)] = low
        kept = jnp.where((source_slot >= 96) & (source_slot < 112), matrix[48:64], 0.0)
        tw_value = tw_value + pltpu.roll(kept, (16 * k - 96) % LANES, 1)
    tw[...] = tw_value
    halves = [pl.ds(0, 8), pl.ds(8, 8)]

    loads[6].wait()
    loads[7].wait()
    lane64, node64 = iota((64, LANES), 1), iota((64, LANES), 0)
    lane_z = lane64 & 15
    node_c = node64 & 3
    for p in range(2):
        for r in range(2):
            columns = pl.ds(r * LANES, LANES)
            rh[p, :, columns] = rhs_v[p, r]
            own = u_v[p, r].astype(F32)
            z_flag = meta[pl.ds(8 + p * 2 + r, 1), :]
            front = jnp.where(lane_z > 0, pltpu.roll(own, 1, 1), 0.0) * (1.0 - z_flag)
            back = jnp.where(lane_z < 15, pltpu.roll(own, LANES - 1, 1), 0.0) * z_flag
            z_source = jnp.where(node_c == 3, front, jnp.where(node_c == 0, back, 0.0))
            src[p, pl.ds(32, 64), columns] = z_source.astype(BF16)
            src[p, pl.ds(96, 32), columns] = jnp.zeros((32, LANES), BF16)

    def settle_y(semaphore):
        @pl.when(has_below & has_above)
        def _():
            settle(semaphore, halo)

        @pl.when(jnp.logical_not(has_below & has_above))
        def _():
            settle(semaphore, halo.at[0])

    settle_y(halo_rs)

    @pl.when(x < xd - 2)
    def _():
        pl.semaphore_wait(know_x.at[0], 1)

    @pl.when((x > 0) & (x < xd - 2))
    def _():
        pl.semaphore_signal(know_x.at[1], inc=1, device_id=at(dx=-1), device_id_type=MESH)

    got_below, got_above = halo[0].astype(F32), halo[1].astype(F32)
    for p in range(2):
        for r in range(2):
            y_flag = meta[pl.ds(4 + p * 2 + r, 1), :]
            m_below, m_above = 1.0 - y_flag, y_flag
            if r == 0:
                other = u_v[p, 1].astype(F32)
            else:
                other = u_v[p, 0].astype(F32)
            pieces = []
            for a_ in range(4):
                tile_rows = slice(8 * a_, 8 * a_ + 8)
                if r == 0:
                    below = pltpu.roll(got_below[tile_rows], 4, 0) if p == 0 else got_below[tile_rows]
                    above = other[16 * a_ : 16 * a_ + 8]
                else:
                    below = other[16 * a_ + 8 : 16 * a_ + 16]
                    above = got_above[tile_rows] if p == 0 else pltpu.roll(got_above[tile_rows], 4, 0)
                pieces.append(jnp.where(sub8 < 4, above * m_above, below * m_below))
            src[p, pl.ds(0, 32), pl.ds(r * LANES, LANES)] = jnp.concatenate(pieces, axis=0).astype(BF16)

    inv_high_out = ih[:, 48:64, :].reshape(NCLASS * 16, 64)
    inv_low_out = il[:, 48:64, :].reshape(NCLASS * 16, 64)
    lat_out = mhl[:, 48:64, :].reshape(NCLASS * 16, 2 * LANES)

    def class_masks(p, r, rows):
        labels = jnp.broadcast_to(meta[pl.ds(p * 2 + r, 1), :], (rows, LANES))
        return [labels == float(k) for k in range(NCLASS)]

    for p in range(2):
        source = src[p]
        stacked = (
            jnp.dot(lat_out, jnp.concatenate([source, source], axis=0), preferred_element_type=F32)
            + jnp.dot(inv_high_out, rh[p], preferred_element_type=F32)
            + jnp.dot(inv_low_out, rh[p], preferred_element_type=F32)
        )
        for r in range(2):
            wo[p, r] = pick_class(stacked[:, r * LANES : (r + 1) * LANES], 16, class_masks(p, r, 16))

    def class_step(index_row, source_ref):
        base = (jnp.broadcast_to(meta[pl.ds(index_row, 1), :], (8, LANES)) * 16.0).astype(jnp.int32)
        sums = [[], []]
        for m in range(16):
            value = spread(source_ref, m)
            for half in range(2):
                sums[half].append(lanes_of(tw[halves[half], :], base + m) * value)
        return total_of(sums[0]), total_of(sums[1])

    for r in range(2):
        parts = class_step(2 + r, wo.at[0, r])
        for half in range(2):
            ob[0, r, halves[half], :] = parts[half] + wo[1, r, halves[half], :]

    pl.semaphore_wait(know.at[0], 2)
    for step in own_steps[:2]:
        send_o(0, step)
    for step in (5, -5):
        send_cls(0, step)

    lane8 = iota((8, LANES), 1)
    pair_first, pair_second = ((lane8 >> 3) & 7) * 16, (lane8 & 7) * 16
    for m in range(16):
        for half in range(2):
            c1s[m, halves[half], :] = lanes_of(tw[halves[half], :], pair_second + m)
            t0s[m, halves[half], :] = lanes_of(tw[halves[half], :], pair_first + m)
    lane16 = iota((16, LANES), 1)

    def pair_product(jj, carry):
        sums = [[], []]
        for m in range(16):
            value = spread(t0s.at[jj], m)
            for half in range(2):
                sums[half].append(c1s[m, halves[half], :] * value)
        product = jnp.concatenate([total_of(sums[0]), total_of(sums[1])], axis=0)
        high = product.astype(BF16)
        rest = product - high.astype(F32)
        middle = rest.astype(BF16)
        low = (rest - middle.astype(F32)).astype(BF16)
        pairs[jj, :, pl.ds(0, LANES)] = jnp.where(lane16 < 64, high.astype(F32), middle.astype(F32)).astype(BF16)
        pairs[jj, :, pl.ds(LANES, LANES)] = jnp.where(lane16 < 64, low.astype(F32), 0.0).astype(BF16)
        return carry

    lax.fori_loop(0, 16, pair_product, 0)

    settle(cls_rs.at[0], clsb.at[pl.ds(0, 4)])
    for held in (2, zd - 2, 1, zd - 1):
        for step in (5, -5):
            if (held + step) % zd not in filled["cls"]:
                send_cls(held, step)
    def full_planes(p, carry):
        source = src[p]
        both = jnp.concatenate([source, source], axis=0)
        stacked = (
            jnp.dot(mhl[...].reshape(NCLASS * 64, 2 * LANES), both, preferred_element_type=F32)
            + jnp.dot(ih[...].reshape(NCLASS * 64, 64), rh[p], preferred_element_type=F32)
            + jnp.dot(il[...].reshape(NCLASS * 64, 64), rh[p], preferred_element_type=F32)
        )
        for r in range(2):
            labels = jnp.broadcast_to(meta[pl.ds(p * 2 + r, 1), :], (64, LANES))
            out_ref[p, r] = pick_class(stacked[:, r * LANES : (r + 1) * LANES], 64, [labels == float(k) for k in range(NCLASS)])
        return carry

    lax.fori_loop(0, 2, full_planes, 0)

    pair_rows = iota((64, LANES), 0)
    lane_low = lane8 & 15

    def propagators(slots):
        for d in slots:
            hot = []
            for r in range(2):
                labels = lanes_of(jnp.broadcast_to(clsb[d], (8, LANES)), lane_low + 16 * r)
                hot.append((jnp.concatenate([labels] * 8, axis=0).astype(jnp.int32) == pair_rows).astype(F32).astype(BF16))
            one = jnp.concatenate(hot, axis=1)
            every = jnp.dot(pairs[...].reshape(256, 2 * LANES), jnp.concatenate([one, one, one, one], axis=0), preferred_element_type=F32)
            for r in range(2):
                ec[d, r] = every[:, r * LANES : (r + 1) * LANES].reshape(16, 16, LANES)

    settle(cls_rs.at[2], clsb.at[3])
    send_cls(3, 5)
    for step in own_steps[2:]:
        send_o(0, step)
    assert len(filled["cls"]) == zd - 1
    propagators((0, 1, 15, 2, 14))
    for r, (held, steps) in enumerate(relays.items()):
        settle(o_rs.at[r], ob.at[held])
        halves_of_8[r].start()
        for step in steps:
            send_o(held, step)
    middle = (3, 5, 11, 4, 12, 6, 10, 7, 9, 13)
    settle(cls_rs.at[1], clsb.at[pl.ds(0, len(middle) - 1)])
    propagators(middle)
    settle(cls_rs.at[3], clsb.at[8])
    propagators((8,))

    def unit_step(i, carry):
        d = lax.rem(z - i + zd, zd)
        for r in range(2):
            sums = [[[] for _ in range(2)] for _ in range(2)]
            for m in range(16):
                values = [spread(up.at[i, r, h], m) for h in range(2)]
                for half in range(2):
                    factor = ec[d, r, m, halves[half], :]
                    for h in range(2):
                        sums[h][half].append(factor * values[h])
            for h in range(2):
                for half in range(2):
                    up[i + 1, r, h, halves[half], :] = total_of(sums[h][half])
        return carry

    for r in range(2):
        for h in range(2):
            up[0, r, h] = (iota((16, LANES), 0) == (lane16 >> 4) + 8 * h).astype(F32)
    lax.fori_loop(0, zd, unit_step, 0)

    @pl.when(x < xd - 3)
    def _():
        pl.semaphore_wait(know_x.at[1], 1)

    px_copies = [
        pltpu.make_async_remote_copy(up.at[zd], px.at[d - 1], px_ss, px_rs, device_id=at(dx=d), device_id_type=MESH)
        for d in range(1, xd)
    ]
    for d in range(1, xd):

        @pl.when(x + d < xd)
        def _(d=d):
            px_copies[d - 1].start()


    def expand(value_ref, slot):
        for r in range(2):
            for h in range(2):
                for half in range(2):
                    whole = value_ref[r, h, halves[half], :]
                    for unit in range(8):
                        ex[slot, r, 8 * h + unit, halves[half], :] = lanes_of(whole, lane_low + 16 * unit)


    def apply(factors, source):
        sums = [[], []]
        for m in range(16):
            value = spread(source, m)
            for half in range(2):
                sums[half].append(factors[m, halves[half], :] * value)
        return total_of(sums[0]), total_of(sums[1])

    assert len(filled["o"]) == zd - 2
    settle(o_rs.at[2], ob.at[pl.ds(0, zd - 3)])
    vp[0] = jnp.zeros((2, 16, LANES), F32)

    def group_step(i, carry):
        d = lax.rem(z - i + zd, zd)
        for r in range(2):
            parts = apply(ec.at[d, r], vp.at[i, r])
            for half in range(2):
                vp[i + 1, r, halves[half], :] = parts[half] + ob[d, r, halves[half], :]
        return carry

    lax.fori_loop(0, zd, group_step, 0)
    xo_copies = [
        pltpu.make_async_remote_copy(vp.at[zd], xo.at[d - 1], xo_ss, xo_rs, device_id=at(dx=d), device_id_type=MESH)
        for d in range(1, xd)
    ]
    for d in range(1, xd):

        @pl.when(x + d < xd)
        def _(d=d):
            xo_copies[d - 1].start()

    expand(up.at[z], xd - 1)
    def settle_x(send_sem, recv_sem, ref):
        for n in range(1, xd):

            @pl.when(x == xd - 1 - n)
            def _(n=n):
                settle(send_sem, ref.at[pl.ds(0, n)])

            @pl.when(x == n)
            def _(n=n):
                settle(recv_sem, ref.at[pl.ds(0, n)])

    settle_x(px_ss, px_rs, px)

    def expand_slot(d, carry):
        expand(px.at[d], d)
        return carry

    lax.fori_loop(0, x, expand_slot, 0)
    xp[0] = inflow_v[...]
    settle_x(xo_ss, xo_rs, xo)

    def x_step(i, carry):
        d = x - i - 1
        for r in range(2):
            parts = apply(ex.at[d, r], xp.at[i, r])
            for half in range(2):
                xp[i + 1, r, halves[half], :] = parts[half] + xo[d, r, halves[half], :]
        return carry

    lax.fori_loop(0, x, x_step, 0)
    for r in range(2):
        parts = apply(ex.at[xd - 1, r], xp.at[x, r])
        for half in range(2):
            ent[r, halves[half], :] = parts[half] + vp[z, r, halves[half], :]
    for r in range(2):
        parts = class_step(r, ent.at[r])
        for half in range(2):
            tr1[r, halves[half], :] = parts[half] + wo[0, r, halves[half], :]

    for p, trace in enumerate((ent, tr1)):
        high, low = high_low(jnp.concatenate([trace[0], trace[1]], axis=1))
        half_rows = jnp.concatenate([jnp.zeros((96, 2 * LANES), BF16), high, low], axis=0)
        stacked = jnp.dot(mhl[...].reshape(NCLASS * 64, 2 * LANES), jnp.concatenate([half_rows, half_rows], axis=0), preferred_element_type=F32)
        for r in range(2):
            out_ref[p, r] = out_ref[p, r] + pick_class(stacked[:, r * LANES : (r + 1) * LANES], 64, class_masks(p, r, 64))

    settle_y(halo_ss)
    settle(cls_ss, clsb.at[pl.ds(0, zd - 1)])
    settle(o_ss, ob.at[pl.ds(0, zd - 1)])


def solution(mesh):
    gxs, yd = mesh.shape["gx"], mesh.shape["gy"]
    zd = min(16, gxs // 2)
    xd = gxs // zd

    def on_device(u_old, rhs, classes, flags, inverse, x_face, lateral_faces, inflow):
        any_space = pl.BlockSpec(memory_space=pl.ANY)
        dma = pltpu.SemaphoreType.DMA
        return pl.pallas_call(
            functools.partial(kernel, xd, zd, yd),
            name="sweep",
            out_shape=pltpu.VMEM((2, 2, 64, LANES), F32),
            in_specs=[any_space] * 8,
            out_specs=pl.BlockSpec(memory_space=pltpu.VMEM),
            scratch_shapes=[
                pltpu.VMEM((2, 2, 64, LANES), BF16),
                pltpu.VMEM((2, 2, 64, LANES), BF16),
                pltpu.VMEM((2, 2, NZ), jnp.int32),
                pltpu.VMEM((2, 2, 2, NZ), jnp.int32),
                pltpu.VMEM((NCLASS, 64, 64), F32),
                pltpu.VMEM((NCLASS, 16, 16), F32),
                pltpu.VMEM((4, NCLASS, 16, 16), F32),
                pltpu.VMEM((2, 16, LANES), F32),
                pltpu.VMEM((2, 32, LANES), BF16),
                pltpu.VMEM((2, 32, LANES), BF16),
                pltpu.VMEM((16, LANES), F32),
                pltpu.VMEM((16, LANES), F32),
                pltpu.VMEM((NCLASS, 64, 64), BF16),
                pltpu.VMEM((NCLASS, 64, 64), BF16),
                pltpu.VMEM((NCLASS, 64, 2 * LANES), BF16),
                pltpu.VMEM((16, LANES), F32),
                pltpu.VMEM((16, 16, LANES), F32),
                pltpu.VMEM((16, 16, LANES), F32),
                pltpu.VMEM((16, 16, 2 * LANES), BF16),
                pltpu.VMEM((2, LANES, 2 * LANES), BF16),
                pltpu.VMEM((2, 64, 2 * LANES), BF16),
                pltpu.VMEM((2, 2, 16, LANES), F32),
                pltpu.VMEM((zd, 1, LANES), F32),
                pltpu.VMEM((zd, 2, 16, LANES), F32),
                pltpu.VMEM((zd, 2, 16, 16, LANES), F32),
                pltpu.VMEM((zd + 1, 2, 2, 16, LANES), F32),
                pltpu.VMEM((zd + 1, 2, 16, LANES), F32),
                pltpu.VMEM((xd - 1, 2, 2, 16, LANES), F32),
                pltpu.VMEM((xd - 1, 2, 16, LANES), F32),
                pltpu.VMEM((xd, 2, 16, 16, LANES), F32),
                pltpu.VMEM((xd, 2, 16, LANES), F32),
                pltpu.VMEM((2, 16, LANES), F32),
                pltpu.VMEM((2, 16, LANES), F32),
                pltpu.SemaphoreType.REGULAR((1,)),
                pltpu.SemaphoreType.REGULAR((2,)),
                dma((8,)),
                dma,
                dma,
                dma,
                dma((4,)),
                dma,
                dma((3,)),
                dma,
                dma,
                dma,
                dma,
            ],
            compiler_params=pltpu.CompilerParams(collective_id=0, has_side_effects=True),
        )(u_old, rhs, classes, flags, inverse, x_face, lateral_faces, inflow)

    return jax.shard_map(
        on_device,
        mesh=mesh,
        in_specs=(
            P("gx", "gy", None, None),
            P("gx", "gy", None, None),
            P("gx", "gy", None),
            P(None, "gx", "gy", None),
            P(),
            P(),
            P(),
            P("gy", None, None),
        ),
        out_specs=P("gx", "gy", None, None),
        check_vma=False,
    )
```

```python
import functools

import jax
import jax.numpy as jnp
from jax import lax
from jax.experimental import pallas as pl
from jax.experimental.pallas import tpu as pltpu
from jax.sharding import PartitionSpec as P

MESH = pl.DeviceIdType.MESH
NCLASS = 8
NZ = 16
LANES = 128
F32 = jnp.float32
BF16 = jnp.bfloat16
HIGHEST = lax.Precision.HIGHEST


def gather_plan(ring):
    assert ring == 16
    own = (5, -5, 3, -3, 2, -2, 1, -1)
    relays = {5: (2, 1, -1), 11: (-2, -1, 1)}
    covered = {0, 8} | {step % ring for step in own} | {(held + step) % ring for held, steps in relays.items() for step in steps}
    assert covered == set(range(ring)), covered
    return own, relays


def iota(shape, axis):
    return lax.broadcasted_iota(jnp.int32, shape, axis)


def lanes_of(value, index):
    return jnp.take_along_axis(value, index, axis=1, mode="promise_in_bounds")


def spread(ref, row):
    return jnp.broadcast_to(ref[pl.ds(row, 1), :], (8, LANES))


def total_of(terms):
    while len(terms) > 1:
        terms = [sum(terms[i : i + 2]) for i in range(0, len(terms), 2)]
    return terms[0]


def high_low(value):
    high = value.astype(BF16)
    return high, (value - high.astype(F32)).astype(BF16)


def pick_class(stacked, rows, masks):
    result = stacked[0:rows]
    for k in range(1, NCLASS):
        result = jnp.where(masks[k], stacked[k * rows : (k + 1) * rows], result)
    return result


def kernel(
    xd, zd, yd,
    u_hbm, rhs_hbm, cls_hbm, flg_hbm, inv_hbm, xf_hbm, lat_hbm, inflow_hbm,
    out_ref,
    u_v, rhs_v, cls_v, flg_v, inv_v, xf_v, lat_v, inflow_v, border, halo,
    meta_in, meta, ih, il, mhl, tw, c1s, t0s, pairs, src, rh, wo,
    clsb, ob, ec, own, up, vp, px, xo, ex, xp, ent, tr1,
    know, know_x, local_sem, halo_ss, halo_rs, cls_ss, cls_rs, o_ss, o_rs, px_ss, px_rs, xo_ss, xo_rs,
):
    gx, gy = lax.axis_index("gx"), lax.axis_index("gy")
    x, z = gx // zd, lax.rem(gx, zd)

    def at(dx=0, dz=0, dy=0):
        gx_to = lax.rem(x + dx + xd, xd) * zd + lax.rem(z + dz + zd, zd)
        return (gx_to, lax.rem(gy + dy + yd, yd))

    own_steps, relays = gather_plan(zd)
    barrier = pltpu.get_barrier_semaphore()
    for d in (3, -3, 2, -2, 1, -1):
        pl.semaphore_signal(barrier, inc=1, device_id=at(dz=d), device_id_type=MESH)
    has_below, has_above = gy > 0, gy < yd - 1

    @pl.when(has_above)
    def _():
        pl.semaphore_signal(barrier, inc=1, device_id=at(dy=1), device_id_type=MESH)

    @pl.when(has_below)
    def _():
        pl.semaphore_signal(barrier, inc=1, device_id=at(dy=-1), device_id_type=MESH)

    @pl.when(x > 0)
    def _():
        pl.semaphore_signal(barrier, inc=1, device_id=at(dx=-1), device_id_type=MESH)

    @pl.when(x < xd - 1)
    def _():
        pl.semaphore_signal(barrier, inc=1, device_id=at(dx=1), device_id_type=MESH)

    greeted = 6 + sum(jnp.where(there, 1, 0) for there in (has_below, has_above, x > 0, x < xd - 1))
    loads = [
        pltpu.make_async_copy(a, b, local_sem.at[i])
        for i, (a, b) in enumerate(
            [(cls_hbm, cls_v), (flg_hbm, flg_v), (u_hbm, u_v), (inv_hbm, inv_v), (lat_hbm, lat_v), (xf_hbm, xf_v), (rhs_hbm, rhs_v), (inflow_hbm, inflow_v)]
        )
    ]
    for load in loads:
        load.start()

    def settle(semaphore, ref):
        pltpu.make_async_copy(ref, ref, semaphore).wait()

    def tell(semaphore, step):
        for sign in (1, -1):
            pl.semaphore_signal(semaphore, inc=1, device_id=at(dz=sign * step), device_id_type=MESH)

    meta_in[...] = jnp.zeros_like(meta_in)
    loads[0].wait()
    loads[1].wait()
    for p in range(2):
        for r in range(2):
            meta_in[pl.ds(p * 2 + r, 1), pl.ds(0, NZ)] = cls_v[p, pl.ds(r, 1), :].astype(F32)
            for f in range(2):
                meta_in[pl.ds(4 + f * 4 + p * 2 + r, 1), pl.ds(0, NZ)] = flg_v[f, p, pl.ds(r, 1), :].astype(F32)
    row, col = iota((LANES, LANES), 0), iota((LANES, LANES), 1)
    tile = ((row < NZ) & (row == (col & 15))).astype(BF16)
    meta_value = jnp.dot(meta_in[...].astype(BF16), tile, preferred_element_type=F32)
    meta[...] = meta_value
    pair = meta_value[0:2] * 8.0 + meta_value[2:4]
    clsb[0] = jnp.where(iota((1, LANES), 1) < NZ, pair[0:1], pair[1:2])

    loads[2].wait()
    sub8 = iota((8, LANES), 0)
    top = [u_v[p, 1].astype(F32) for p in range(2)]
    bottom = [u_v[p, 0].astype(F32) for p in range(2)]
    packed_top, packed_bottom = [], []
    for a_ in range(4):
        low_rows, high_rows = slice(16 * a_, 16 * a_ + 8), slice(16 * a_ + 8, 16 * a_ + 16)
        packed_top.append(jnp.where(sub8 < 4, pltpu.roll(top[0][high_rows], 4, 0), top[1][high_rows]))
        packed_bottom.append(jnp.where(sub8 < 4, bottom[0][low_rows], pltpu.roll(bottom[1][low_rows], 4, 0)))
    border[0] = jnp.concatenate(packed_top, axis=0).astype(BF16)
    border[1] = jnp.concatenate(packed_bottom, axis=0).astype(BF16)
    pl.semaphore_wait(barrier, greeted)

    tell(know.at[0], 2)

    halo_copies = [
        pltpu.make_async_remote_copy(border.at[0], halo.at[0], halo_ss, halo_rs, device_id=at(dy=1), device_id_type=MESH),
        pltpu.make_async_remote_copy(border.at[1], halo.at[1], halo_ss, halo_rs, device_id=at(dy=-1), device_id_type=MESH),
    ]
    @pl.when(has_above)
    def _():
        halo_copies[0].start()

    @pl.when(has_below)
    def _():
        halo_copies[1].start()

    @pl.when(gy == 0)
    def _():
        halo[0] = jnp.zeros((32, LANES), BF16)

    @pl.when(gy == yd - 1)
    def _():
        halo[1] = jnp.zeros((32, LANES), BF16)

    @pl.when((x > 0) & (x < xd - 1))
    def _():
        pl.semaphore_signal(know_x.at[0], inc=1, device_id=at(dx=-1), device_id_type=MESH)

    near_steps = (2, -2, 3, 1, -1)
    filled = {"cls": [], "o": []}

    def send_cls(held, step):
        to = (held + step) % zd
        assert to not in filled["cls"]
        filled["cls"].append(to)
        arrival = cls_rs.at[{3: 2, 8: 3}.get(to, 0 if held == 0 and step in near_steps else 1)]
        pltpu.make_async_remote_copy(clsb.at[held], clsb.at[to], cls_ss, arrival, device_id=at(dz=step), device_id_type=MESH).start()

    def send_o(held, step):
        to = (held + step) % zd
        assert to not in filled["o"]
        filled["o"].append(to)
        arrival = o_rs.at[0 if to == 5 else 1 if to == 11 else 2]
        pltpu.make_async_remote_copy(ob.at[held], ob.at[to], o_ss, arrival, device_id=at(dz=step), device_id_type=MESH).start()

    for step in near_steps:
        send_cls(0, step)
    halves_of_8 = [
        pltpu.make_async_remote_copy(ob.at[held, r], ob.at[8, r], o_ss, o_rs.at[2], device_id=at(dz=step), device_id_type=MESH)
        for r, (held, step) in enumerate([(5, 3), (11, -3)])
    ]

    loads[3].wait()
    loads[4].wait()
    loads[5].wait()
    inv_all = inv_v[...].reshape(NCLASS * 64, 64)
    ih_value, il_value = high_low(inv_all)
    ih[...] = ih_value.reshape(NCLASS, 64, 64)
    il[...] = il_value.reshape(NCLASS, 64, 64)
    node, slot = iota((64, LANES), 0), iota((64, LANES), 1)
    face, j = slot >> 4, slot & 15
    a, b = j >> 2, j & 3
    y_node = 16 * a + b
    wanted = jnp.where(face == 0, y_node, jnp.where(face == 1, y_node + 12, jnp.where(face == 2, 4 * j, jnp.where(face == 3, 4 * j + 3, jnp.where(face == 4, j, -1)))))
    faces_of = jnp.dot(inv_all, (node == wanted).astype(F32), precision=HIGHEST, preferred_element_type=F32)
    tables = jnp.concatenate([lat_v[...].reshape(4 * NCLASS * 16, 16), xf_v[...].reshape(NCLASS * 16, 16)], axis=0)
    source_slot, sj = iota((16, LANES), 1), iota((16, LANES), 0)

    def slot_face_and_j(s):
        y_face = jnp.where((s & 7) < 4, 1, 0)
        y_j = 4 * (s >> 3) + (s & 3)
        t = s - 32
        z_face = jnp.where((t & 3) == 3, 2, jnp.where((t & 3) == 0, 3, -1))
        z_j = t >> 2
        in_face = jnp.where(s < 32, y_face, jnp.where(s < 96, z_face, 4))
        in_j = jnp.where(s < 32, y_j, jnp.where(s < 96, z_j, s & 15))
        return in_face, in_j

    slot_face, column_j = slot_face_and_j(source_slot)
    placed = jnp.dot(tables, (column_j == sj).astype(F32), precision=HIGHEST, preferred_element_type=F32)
    tw_value = jnp.zeros((16, LANES), F32)
    for k in range(NCLASS):
        blocks = []
        for f in range(5):
            start = (f * NCLASS + k) * 16
            blocks.append(jnp.where(slot_face == f, placed[start : start + 16], 0.0))
        blocks.append(jnp.zeros((48, LANES), F32))
        matrix = -jnp.dot(faces_of[k * 64 : (k + 1) * 64], jnp.concatenate(blocks, axis=0), precision=HIGHEST, preferred_element_type=F32)
        high, low = high_low(matrix)
        mhl[k, :, pl.ds(0, LANES)] = high
        mhl[k, :, pl.ds(LANES, LANES)] = low
        kept = jnp.where((source_slot >= 96) & (source_slot < 112), matrix[48:64], 0.0)
        tw_value = tw_value + pltpu.roll(kept, (16 * k - 96) % LANES, 1)
    tw[...] = tw_value
    halves = [pl.ds(0, 8), pl.ds(8, 8)]

    for p in range(2):
        for r in range(2):
            base = (jnp.broadcast_to(meta[pl.ds(p * 2 + r, 1), :], (8, LANES)) * 16.0).astype(jnp.int32)
            for m in range(16):
                for half in range(2):
                    own[p, r, m, halves[half], :] = lanes_of(tw_value[half * 8 : half * 8 + 8], base + m)

    loads[6].wait()
    loads[7].wait()
    lane64, node64 = iota((64, LANES), 1), iota((64, LANES), 0)
    lane_z = lane64 & 15
    node_c = node64 & 3
    for p in range(2):
        for r in range(2):
            columns = pl.ds(r * LANES, LANES)
            rh[p, :, columns] = rhs_v[p, r]
            here = u_v[p, r].astype(F32)
            z_flag = meta[pl.ds(8 + p * 2 + r, 1), :]
            front = jnp.where(lane_z > 0, pltpu.roll(here, 1, 1), 0.0) * (1.0 - z_flag)
            back = jnp.where(lane_z < 15, pltpu.roll(here, LANES - 1, 1), 0.0) * z_flag
            z_source = jnp.where(node_c == 3, front, jnp.where(node_c == 0, back, 0.0))
            src[p, pl.ds(32, 64), columns] = z_source.astype(BF16)
            src[p, pl.ds(96, 32), columns] = jnp.zeros((32, LANES), BF16)

    def settle_y(semaphore):
        @pl.when(has_below & has_above)
        def _():
            settle(semaphore, halo)

        @pl.when(jnp.logical_not(has_below & has_above))
        def _():
            settle(semaphore, halo.at[0])

    settle_y(halo_rs)

    @pl.when(x < xd - 2)
    def _():
        pl.semaphore_wait(know_x.at[0], 1)

    @pl.when((x > 0) & (x < xd - 2))
    def _():
        pl.semaphore_signal(know_x.at[1], inc=1, device_id=at(dx=-1), device_id_type=MESH)

    got_below, got_above = halo[0].astype(F32), halo[1].astype(F32)
    for p in range(2):
        for r in range(2):
            y_flag = meta[pl.ds(4 + p * 2 + r, 1), :]
            m_below, m_above = 1.0 - y_flag, y_flag
            if r == 0:
                other = u_v[p, 1].astype(F32)
            else:
                other = u_v[p, 0].astype(F32)
            pieces = []
            for a_ in range(4):
                tile_rows = slice(8 * a_, 8 * a_ + 8)
                if r == 0:
                    below = pltpu.roll(got_below[tile_rows], 4, 0) if p == 0 else got_below[tile_rows]
                    above = other[16 * a_ : 16 * a_ + 8]
                else:
                    below = other[16 * a_ + 8 : 16 * a_ + 16]
                    above = got_above[tile_rows] if p == 0 else pltpu.roll(got_above[tile_rows], 4, 0)
                pieces.append(jnp.where(sub8 < 4, above * m_above, below * m_below))
            src[p, pl.ds(0, 32), pl.ds(r * LANES, LANES)] = jnp.concatenate(pieces, axis=0).astype(BF16)

    inv_high_out = ih[:, 48:64, :].reshape(NCLASS * 16, 64)
    inv_low_out = il[:, 48:64, :].reshape(NCLASS * 16, 64)
    lat_out = mhl[:, 48:64, :].reshape(NCLASS * 16, 2 * LANES)

    def class_masks(p, r, rows):
        labels = jnp.broadcast_to(meta[pl.ds(p * 2 + r, 1), :], (rows, LANES))
        return [labels == float(k) for k in range(NCLASS)]

    for p in range(2):
        source = src[p]
        stacked = (
            jnp.dot(lat_out, jnp.concatenate([source, source], axis=0), preferred_element_type=F32)
            + jnp.dot(inv_high_out, rh[p], preferred_element_type=F32)
            + jnp.dot(inv_low_out, rh[p], preferred_element_type=F32)
        )
        for r in range(2):
            wo[p, r] = pick_class(stacked[:, r * LANES : (r + 1) * LANES], 16, class_masks(p, r, 16))

    def apply(factors, source):
        sums = [[], []]
        for m in range(16):
            value = spread(source, m)
            for half in range(2):
                sums[half].append(factors[m, halves[half], :] * value)
        return total_of(sums[0]), total_of(sums[1])

    for r in range(2):
        parts = apply(own.at[1, r], wo.at[0, r])
        for half in range(2):
            ob[0, r, halves[half], :] = parts[half] + wo[1, r, halves[half], :]

    pl.semaphore_wait(know.at[0], 2)
    for step in own_steps[:2]:
        send_o(0, step)
    for step in (5, -5):
        send_cls(0, step)

    lane8 = iota((8, LANES), 1)
    pair_first, pair_second = ((lane8 >> 3) & 7) * 16, (lane8 & 7) * 16
    for m in range(16):
        for half in range(2):
            c1s[m, halves[half], :] = lanes_of(tw[halves[half], :], pair_second + m)
            t0s[m, halves[half], :] = lanes_of(tw[halves[half], :], pair_first + m)
    lane16 = iota((16, LANES), 1)

    def pair_product(jj, carry):
        sums = [[], []]
        for m in range(16):
            value = spread(t0s.at[jj], m)
            for half in range(2):
                sums[half].append(c1s[m, halves[half], :] * value)
        product = jnp.concatenate([total_of(sums[0]), total_of(sums[1])], axis=0)
        high = product.astype(BF16)
        rest = product - high.astype(F32)
        middle = rest.astype(BF16)
        low = (rest - middle.astype(F32)).astype(BF16)
        pairs[jj, :, pl.ds(0, LANES)] = jnp.where(lane16 < 64, high.astype(F32), middle.astype(F32)).astype(BF16)
        pairs[jj, :, pl.ds(LANES, LANES)] = jnp.where(lane16 < 64, low.astype(F32), 0.0).astype(BF16)
        return carry

    lax.fori_loop(0, 16, pair_product, 0)

    settle(cls_rs.at[0], clsb.at[pl.ds(0, 4)])
    for held in (2, zd - 2, 1, zd - 1):
        for step in (5, -5):
            if (held + step) % zd not in filled["cls"]:
                send_cls(held, step)
    def full_planes(p, carry):
        source = src[p]
        both = jnp.concatenate([source, source], axis=0)
        stacked = (
            jnp.dot(mhl[...].reshape(NCLASS * 64, 2 * LANES), both, preferred_element_type=F32)
            + jnp.dot(ih[...].reshape(NCLASS * 64, 64), rh[p], preferred_element_type=F32)
            + jnp.dot(il[...].reshape(NCLASS * 64, 64), rh[p], preferred_element_type=F32)
        )
        for r in range(2):
            labels = jnp.broadcast_to(meta[pl.ds(p * 2 + r, 1), :], (64, LANES))
            out_ref[p, r] = pick_class(stacked[:, r * LANES : (r + 1) * LANES], 64, [labels == float(k) for k in range(NCLASS)])
        return carry

    lax.fori_loop(0, 2, full_planes, 0)

    pair_rows = iota((64, LANES), 0)
    lane_low = lane8 & 15

    def propagators(slots):
        for d in slots:
            hot = []
            for r in range(2):
                labels = lanes_of(jnp.broadcast_to(clsb[d], (8, LANES)), lane_low + 16 * r)
                hot.append((jnp.concatenate([labels] * 8, axis=0).astype(jnp.int32) == pair_rows).astype(F32).astype(BF16))
            one = jnp.concatenate(hot, axis=1)
            every = jnp.dot(pairs[...].reshape(256, 2 * LANES), jnp.concatenate([one, one, one, one], axis=0), preferred_element_type=F32)
            for r in range(2):
                ec[d, r] = every[:, r * LANES : (r + 1) * LANES].reshape(16, 16, LANES)

    settle(cls_rs.at[2], clsb.at[3])
    send_cls(3, 5)
    for step in own_steps[2:4]:
        send_o(0, step)
    assert len(filled["cls"]) == zd - 1
    propagators((0, 1, 15, 2, 14))
    for step in own_steps[4:]:
        send_o(0, step)
    for r, (held, steps) in enumerate(relays.items()):
        settle(o_rs.at[r], ob.at[held])
        halves_of_8[r].start()
        for step in steps:
            send_o(held, step)
    middle = (3, 5, 11, 4, 12, 6, 10, 7, 9, 13)
    settle(cls_rs.at[1], clsb.at[pl.ds(0, len(middle) - 1)])
    propagators(middle)
    settle(cls_rs.at[3], clsb.at[8])
    propagators((8,))

    def unit_step(i, carry):
        d = lax.rem(z - i + zd, zd)
        for r in range(2):
            sums = [[[] for _ in range(2)] for _ in range(2)]
            for m in range(16):
                values = [spread(up.at[i, r, h], m) for h in range(2)]
                for half in range(2):
                    factor = ec[d, r, m, halves[half], :]
                    for h in range(2):
                        sums[h][half].append(factor * values[h])
            for h in range(2):
                for half in range(2):
                    up[i + 1, r, h, halves[half], :] = total_of(sums[h][half])
        return carry

    for r in range(2):
        for h in range(2):
            up[0, r, h] = (iota((16, LANES), 0) == (lane16 >> 4) + 8 * h).astype(F32)
    lax.fori_loop(0, zd, unit_step, 0)

    @pl.when(x < xd - 3)
    def _():
        pl.semaphore_wait(know_x.at[1], 1)

    px_copies = [
        pltpu.make_async_remote_copy(up.at[zd], px.at[d - 1], px_ss, px_rs, device_id=at(dx=d), device_id_type=MESH)
        for d in range(1, xd)
    ]
    for d in range(1, xd):

        @pl.when(x + d < xd)
        def _(d=d):
            px_copies[d - 1].start()


    def expand(value_ref, slot):
        for r in range(2):
            for h in range(2):
                for half in range(2):
                    whole = value_ref[r, h, halves[half], :]
                    for unit in range(8):
                        ex[slot, r, 8 * h + unit, halves[half], :] = lanes_of(whole, lane_low + 16 * unit)


    assert len(filled["o"]) == zd - 2
    settle(o_rs.at[2], ob.at[pl.ds(0, zd - 3)])
    vp[0] = jnp.zeros((2, 16, LANES), F32)

    def group_step(i, carry):
        d = lax.rem(z - i + zd, zd)
        for r in range(2):
            parts = apply(ec.at[d, r], vp.at[i, r])
            for half in range(2):
                vp[i + 1, r, halves[half], :] = parts[half] + ob[d, r, halves[half], :]
        return carry

    lax.fori_loop(0, zd, group_step, 0)
    xo_copies = [
        pltpu.make_async_remote_copy(vp.at[zd], xo.at[d - 1], xo_ss, xo_rs, device_id=at(dx=d), device_id_type=MESH)
        for d in range(1, xd)
    ]
    for d in range(1, xd):

        @pl.when(x + d < xd)
        def _(d=d):
            xo_copies[d - 1].start()

    expand(up.at[z], xd - 1)
    def settle_x(send_sem, recv_sem, ref):
        for n in range(1, xd):

            @pl.when(x == xd - 1 - n)
            def _(n=n):
                settle(send_sem, ref.at[pl.ds(0, n)])

            @pl.when(x == n)
            def _(n=n):
                settle(recv_sem, ref.at[pl.ds(0, n)])

    settle_x(px_ss, px_rs, px)

    def expand_slot(d, carry):
        expand(px.at[d], d)
        return carry

    lax.fori_loop(0, x, expand_slot, 0)
    xp[0] = inflow_v[...]
    settle_x(xo_ss, xo_rs, xo)

    def x_step(i, carry):
        d = x - i - 1
        for r in range(2):
            parts = apply(ex.at[d, r], xp.at[i, r])
            for half in range(2):
                xp[i + 1, r, halves[half], :] = parts[half] + xo[d, r, halves[half], :]
        return carry

    lax.fori_loop(0, x, x_step, 0)
    for r in range(2):
        parts = apply(ex.at[xd - 1, r], xp.at[x, r])
        for half in range(2):
            ent[r, halves[half], :] = parts[half] + vp[z, r, halves[half], :]
    for r in range(2):
        parts = apply(own.at[0, r], ent.at[r])
        for half in range(2):
            tr1[r, halves[half], :] = parts[half] + wo[0, r, halves[half], :]

    for p, trace in enumerate((ent, tr1)):
        high, low = high_low(jnp.concatenate([trace[0], trace[1]], axis=1))
        half_rows = jnp.concatenate([jnp.zeros((96, 2 * LANES), BF16), high, low], axis=0)
        stacked = jnp.dot(mhl[...].reshape(NCLASS * 64, 2 * LANES), jnp.concatenate([half_rows, half_rows], axis=0), preferred_element_type=F32)
        for r in range(2):
            out_ref[p, r] = out_ref[p, r] + pick_class(stacked[:, r * LANES : (r + 1) * LANES], 64, class_masks(p, r, 64))

    settle_y(halo_ss)
    settle(cls_ss, clsb.at[pl.ds(0, zd - 1)])
    settle(o_ss, ob.at[pl.ds(0, zd - 1)])


def solution(mesh):
    gxs, yd = mesh.shape["gx"], mesh.shape["gy"]
    zd = min(16, gxs // 2)
    xd = gxs // zd

    def on_device(u_old, rhs, classes, flags, inverse, x_face, lateral_faces, inflow):
        any_space = pl.BlockSpec(memory_space=pl.ANY)
        dma = pltpu.SemaphoreType.DMA
        return pl.pallas_call(
            functools.partial(kernel, xd, zd, yd),
            name="sweep",
            out_shape=pltpu.VMEM((2, 2, 64, LANES), F32),
            in_specs=[any_space] * 8,
            out_specs=pl.BlockSpec(memory_space=pltpu.VMEM),
            scratch_shapes=[
                pltpu.VMEM((2, 2, 64, LANES), BF16),
                pltpu.VMEM((2, 2, 64, LANES), BF16),
                pltpu.VMEM((2, 2, NZ), jnp.int32),
                pltpu.VMEM((2, 2, 2, NZ), jnp.int32),
                pltpu.VMEM((NCLASS, 64, 64), F32),
                pltpu.VMEM((NCLASS, 16, 16), F32),
                pltpu.VMEM((4, NCLASS, 16, 16), F32),
                pltpu.VMEM((2, 16, LANES), F32),
                pltpu.VMEM((2, 32, LANES), BF16),
                pltpu.VMEM((2, 32, LANES), BF16),
                pltpu.VMEM((16, LANES), F32),
                pltpu.VMEM((16, LANES), F32),
                pltpu.VMEM((NCLASS, 64, 64), BF16),
                pltpu.VMEM((NCLASS, 64, 64), BF16),
                pltpu.VMEM((NCLASS, 64, 2 * LANES), BF16),
                pltpu.VMEM((16, LANES), F32),
                pltpu.VMEM((16, 16, LANES), F32),
                pltpu.VMEM((16, 16, LANES), F32),
                pltpu.VMEM((16, 16, 2 * LANES), BF16),
                pltpu.VMEM((2, LANES, 2 * LANES), BF16),
                pltpu.VMEM((2, 64, 2 * LANES), BF16),
                pltpu.VMEM((2, 2, 16, LANES), F32),
                pltpu.VMEM((zd, 1, LANES), F32),
                pltpu.VMEM((zd, 2, 16, LANES), F32),
                pltpu.VMEM((zd, 2, 16, 16, LANES), F32),
                pltpu.VMEM((2, 2, 16, 16, LANES), F32),
                pltpu.VMEM((zd + 1, 2, 2, 16, LANES), F32),
                pltpu.VMEM((zd + 1, 2, 16, LANES), F32),
                pltpu.VMEM((xd - 1, 2, 2, 16, LANES), F32),
                pltpu.VMEM((xd - 1, 2, 16, LANES), F32),
                pltpu.VMEM((xd, 2, 16, 16, LANES), F32),
                pltpu.VMEM((xd, 2, 16, LANES), F32),
                pltpu.VMEM((2, 16, LANES), F32),
                pltpu.VMEM((2, 16, LANES), F32),
                pltpu.SemaphoreType.REGULAR((1,)),
                pltpu.SemaphoreType.REGULAR((2,)),
                dma((8,)),
                dma,
                dma,
                dma,
                dma((4,)),
                dma,
                dma((3,)),
                dma,
                dma,
                dma,
                dma,
            ],
            compiler_params=pltpu.CompilerParams(collective_id=0, has_side_effects=True),
        )(u_old, rhs, classes, flags, inverse, x_face, lateral_faces, inflow)

    return jax.shard_map(
        on_device,
        mesh=mesh,
        in_specs=(
            P("gx", "gy", None, None),
            P("gx", "gy", None, None),
            P("gx", "gy", None),
            P(None, "gx", "gy", None),
            P(),
            P(),
            P(),
            P("gy", None, None),
        ),
        out_specs=P("gx", "gy", None, None),
        check_vma=False,
    )
```
